128 devices in a mesh: row: 8 (over z, core), col: 16 (over y, x).
Axes of the slice: x: 4, y: 4, z: 4, core: 2. Of those that a mesh axis runs over, the one named last changes fastest.
Arguments:
- a_matrix: float32 [16384, 16384], P('row', 'col'), may hold values from -2.25 to 2.25
- b_matrix: float32 [16384, 16384], P('row', 'col'), may hold values from -0.1 to 3.1
- x_block: float32 [16384, 64], P('row'), may hold values from -6 to 6
- r_block: float32 [16384, 64], P('row'), may hold values from -6 to 6
- p_block: float32 [16384, 64], P('row'), may hold values from -6 to 6
Outputs:
- x_next: float32 [16384, 64], P('row')
- r_next: float32 [16384, 64], P('row')
- p_next: float32 [16384, 64], P('row')
The draws below stay inside these ranges and needn't reach their ends.
All inputs are finite; a program needn't handle non-finite values.
Results may differ from the reference program's by a relative error of at most 0.0003.
Values sent between devices are 32-bit elements; how exact they have to be, the bound alone decides.
No kernel may reach another device: no remote copies, remote signals or barrier semaphores. Data moves between devices by JAX's collectives and lax.ppermute only.
A program may use at most 128 MiB of HBM per device.

```python
import math
import jax
import jax.numpy as jnp
from jax import lax

N = 16384
K = 64
ITERS = 2
NS_STEPS = 8


def symmetric_field(key, spread, low, high):
    keys = jax.random.split(key, 2)
    noise = jax.random.normal(keys[0], (N, N), jnp.float32)
    mixed = (noise + noise.T) * (spread / math.sqrt(2.0 * N))
    diag_vals = jax.random.uniform(keys[1], (N,), jnp.float32, low, high)
    return mixed + jnp.diag(diag_vals)


def draw_a_matrix(key, part):
    return symmetric_field(jax.random.fold_in(key, 11), 0.5, -2.0, 2.0)


def draw_b_matrix(key, part):
    return symmetric_field(jax.random.fold_in(key, 23), 0.3, 1.5, 3.0)


def shard_levels(rng, shape, cuts, low, largest):
    level = 1.0
    for position, shards_of in cuts:
        heights = jax.random.uniform(jax.random.fold_in(jax.random.fold_in(rng, 6), position), (shards_of,), jnp.float32, low / len(cuts), largest / len(cuts))
        level = level * jnp.repeat(jnp.exp(heights), shape[position] // shards_of).reshape((-1,) + (1,) * (len(shape) - 1 - position))
    return level


def normal_values(own_key, shape, scale, most, cuts=(), held_as=jnp.bfloat16):
    entries = scale * jax.random.normal(own_key, shape, jnp.float32)
    if cuts:
        entries = entries * shard_levels(own_key, shape, cuts, -0.22, 0.18)
    return jnp.clip(entries, -most, most).astype(held_as)


def setup_inputs(seed: int = 0) -> dict:
    seeds = jax.random.split(jax.random.key(seed), 6)
    return {
        "a_matrix": draw_a_matrix(jax.random.fold_in(seeds[5], 71), 0),
        "b_matrix": draw_b_matrix(jax.random.fold_in(seeds[5], 71), 0),
        "x_block": normal_values(seeds[2], (N, K), 1.0, 6.0, ((0, 8),), jnp.float32),
        "r_block": normal_values(seeds[3], (N, K), 1.0, 6.0, ((0, 8),), jnp.float32),
        "p_block": normal_values(seeds[4], (N, K), 1.0, 6.0, ((0, 8),), jnp.float32),
    }


def matmul(left, right):
    return jnp.dot(left.astype(jnp.float32), right.astype(jnp.float32), precision=lax.Precision.HIGHEST, preferred_element_type=jnp.float32)

def ritz_step(gram_a, gram_b, count):
    gram_a = 0.5 * (gram_a + gram_a.T)
    gram_b = 0.5 * (gram_b + gram_b.T)
    lower = jnp.linalg.cholesky(gram_b)
    half = lax.linalg.triangular_solve(lower, gram_a, left_side=True, lower=True)
    middle = lax.linalg.triangular_solve(lower, half.T, left_side=True, lower=True)
    middle = 0.5 * (middle + middle.T)
    extent = middle.shape[0]
    ident = jnp.eye(extent, dtype=middle.dtype)
    shift = jnp.trace(middle) / extent
    centred = middle - shift * ident
    sign_est = centred / jnp.sqrt(jnp.sum(centred * centred) + 1e-06)
    for turn in range(NS_STEPS):
        sign_est = 1.5 * sign_est - 0.5 * matmul(sign_est, matmul(sign_est, sign_est))
    filtered = (0.5 * (ident - sign_est))[:, :count]
    coords = lax.linalg.triangular_solve(lower, filtered, left_side=True, lower=True, transpose_a=True) * math.sqrt(N)
    reduced = matmul(filtered.T, matmul(middle, filtered))
    return (coords, reduced)

def reference(a_matrix, b_matrix, x_block, r_block, p_block):
    for turn in range(ITERS):
        panel = jnp.concatenate([x_block, r_block, p_block], axis=1)
        prod_a = matmul(a_matrix, panel)
        prod_b = matmul(b_matrix, panel)
        coords, reduced = ritz_step(matmul(panel.T, prod_a), matmul(panel.T, prod_b), K)
        x_block = matmul(panel, coords)
        p_block = matmul(panel[:, K:], coords[K:])
        r_block = matmul(prod_a, coords) - matmul(matmul(prod_b, coords), reduced)
    return (x_block, r_block, p_block)
```

```python
import math

import jax
import jax.numpy as jnp
from jax import lax
from jax.sharding import PartitionSpec as P

NS_STEPS = 8
BOTH = ("row", "col")


def mm(left, right, dims=((1,), (0,)), precision=lax.Precision.HIGHEST):
    return lax.dot_general(
        left, right, (dims, ((), ())), precision=precision, preferred_element_type=jnp.float32
    )


def share(x, axis):
    copies = jnp.broadcast_to(x[None], (lax.axis_size(axis),) + x.shape)
    return lax.all_to_all(copies, axis, 0, 0)


def sum_everywhere(x):
    parts = x.reshape(lax.axis_size("row"), -1, x.shape[-1])
    own = lax.all_to_all(parts, "row", 0, 0).sum(0)
    own = share(own, "col").sum(0)
    return share(own, "row").reshape(x.shape)


def sides(gram, k):
    return [gram[i * k : (i + 1) * k, j * k : (j + 1) * k] for i in range(3) for j in range(i + 1)]


def whole(blocks):
    b00, b10, b11, b20, b21, b22 = blocks
    return jnp.concatenate(
        [
            jnp.concatenate([b00, b10.T, b20.T], 1),
            jnp.concatenate([b10, b11, b21.T], 1),
            jnp.concatenate([b20, b21, b22], 1),
        ],
        0,
    )


def ritz_step(gram_a, gram_b, count, order):
    lower = jnp.linalg.cholesky(gram_b)
    half = lax.linalg.triangular_solve(lower, gram_a, left_side=True, lower=True)
    middle = lax.linalg.triangular_solve(lower, half.T, left_side=True, lower=True)
    middle = 0.5 * (middle + middle.T)
    extent = middle.shape[0]
    ident = jnp.eye(extent, dtype=middle.dtype)
    shift = jnp.trace(middle) / extent
    centred = middle - shift * ident
    sign_est = centred / jnp.sqrt(jnp.sum(centred * centred) + 1e-06)
    for turn in range(NS_STEPS):
        sign_est = 1.5 * sign_est - 0.5 * mm(sign_est, mm(sign_est, sign_est))
    filtered = (0.5 * (ident - sign_est))[:, :count]
    coords = lax.linalg.triangular_solve(
        lower, filtered, left_side=True, lower=True, transpose_a=True
    ) * math.sqrt(order)
    reduced = mm(filtered.T, mm(middle, filtered))
    return (coords, reduced)


def symmetric(x):
    return 0.5 * (x + x.T)


def local(a_matrix, b_matrix, x_block, r_block, p_block):
    rows, cols = lax.axis_size("row"), lax.axis_size("col")
    count = rows * cols
    k = x_block.shape[1]
    order = x_block.shape[0] * rows
    piece = order // count
    high = lax.Precision.HIGH
    to_col = [(b, (b % rows) * cols + b // rows) for b in range(count)]
    to_row = [(d, s) for s, d in to_col]

    panel = jnp.concatenate([x_block.T, r_block.T, p_block.T], 0)
    start = lax.axis_index("col") * piece
    own_row = lax.dynamic_slice_in_dim(panel, start, piece, 1)
    own_col = lax.ppermute(own_row, BOTH, to_col)

    prods = jnp.concatenate(
        [mm(panel, a_matrix, precision=high), mm(panel, b_matrix, precision=high)], 0
    )
    prods_by_piece = prods.reshape(6 * k, rows, piece).transpose(1, 0, 2)
    prod_col = lax.psum_scatter(prods_by_piece, "row", scatter_dimension=0)
    prod_row = lax.ppermute(prod_col, BOTH, to_row)
    matched = share(own_col, "row").transpose(1, 0, 2).reshape(3 * k, -1)
    grams = mm(prods, matched, ((1,), (1,)), high)
    packed = jnp.concatenate(
        [
            jnp.concatenate([ga, gb], 1)
            for ga, gb in zip(
                sides(symmetric(grams[: 3 * k]), k), sides(symmetric(grams[3 * k :]), k)
            )
        ],
        0,
    )
    packed = sum_everywhere(packed).reshape(6, k, 2 * k)
    gram_a = whole([packed[i, :, :k] for i in range(6)])
    gram_b = whole([packed[i, :, k:] for i in range(6)])
    coords, reduced = ritz_step(gram_a, gram_b, k, order)

    turn = jnp.concatenate([coords, -mm(coords, reduced)], 0)
    resid_col = mm(turn, prod_col, ((0,), (0,)))
    resid_row = mm(turn, prod_row, ((0,), (0,)))
    resid = share(resid_col, "row").transpose(1, 0, 2).reshape(k, -1)
    parts = jnp.concatenate(
        [
            mm(resid, a_matrix, ((1,), (1,)), high),
            mm(resid, b_matrix, ((1,), (1,)), high),
        ],
        0,
    )
    parts = parts.reshape(2 * k, cols, piece).transpose(1, 0, 2)
    more_row = lax.all_to_all(parts, "col", 0, 0).sum(0)

    shift_coords = jnp.concatenate([jnp.zeros_like(coords[:k]), coords[k:]], 0)
    basis = jnp.concatenate([coords, shift_coords], 1)
    kept = mm(basis, own_row, ((0,), (0,)))
    tests = jnp.concatenate([kept[:k], resid_row, kept[k:]], 0)
    fresh = mm(tests, more_row, ((1,), (1,)))
    fresh = sum_everywhere(fresh)
    old_a = symmetric(mm(basis, mm(gram_a, basis), ((0,), (0,))))
    old_b = symmetric(mm(basis, mm(gram_b, basis), ((0,), (0,))))

    def joined(old, new):
        return whole(
            [
                old[:k, :k],
                new[:k].T,
                symmetric(new[k : 2 * k]),
                old[k:, :k],
                new[2 * k :],
                old[k:, k:],
            ]
        )

    coords2, reduced2 = ritz_step(
        joined(old_a, fresh[:, :k]), joined(old_b, fresh[:, k:]), k, order
    )
    from_x, from_r, from_p = coords2[:k], coords2[k : 2 * k], coords2[2 * k :]
    move_p = mm(shift_coords, from_p)
    move_x = mm(coords, from_x) + move_p
    part_r = mm(from_r, resid_row, ((0,), (0,)))
    x_own = mm(move_x, own_row, ((0,), (0,))) + part_r
    p_own = mm(move_p, own_row, ((0,), (0,))) + part_r
    r_own = (
        mm(jnp.concatenate([move_x, -mm(move_x, reduced2)], 0), prod_row, ((0,), (0,)))
        + mm(jnp.concatenate([from_r, -mm(from_r, reduced2)], 0), more_row, ((0,), (0,)))
    )
    outs = share(jnp.concatenate([x_own, r_own, p_own], 0), "col")
    outs = outs.transpose(1, 0, 2).reshape(3 * k, -1)
    return (outs[:k].T, outs[k : 2 * k].T, outs[2 * k :].T)


def solution(mesh):
    return jax.shard_map(
        local,
        mesh=mesh,
        in_specs=(P("row", "col"), P("row", "col"), P("row", None), P("row", None), P("row", None)),
        out_specs=(P("row", None), P("row", None), P("row", None)),
        check_vma=False,
    )
```

```python
import functools
import math

import jax
import jax.numpy as jnp
from jax import lax
from jax.experimental import pallas as pl
from jax.experimental.pallas import tpu as pltpu
from jax.sharding import PartitionSpec as P

NS_STEPS = 8
BOTH = ("row", "col")


def mm(left, right, dims=((1,), (0,)), precision=lax.Precision.HIGHEST):
    return lax.dot_general(
        left, right, (dims, ((), ())), precision=precision, preferred_element_type=jnp.float32
    )


def share(x, axis):
    copies = jnp.broadcast_to(x[None], (lax.axis_size(axis),) + x.shape)
    return lax.all_to_all(copies, axis, 0, 0)


def sum_everywhere(x):
    parts = x.reshape(lax.axis_size("row"), -1, x.shape[-1])
    own = lax.all_to_all(parts, "row", 0, 0).sum(0)
    own = share(own, "col").sum(0)
    return share(own, "row").reshape(x.shape)


def sides(gram, k):
    return [gram[i * k : (i + 1) * k, j * k : (j + 1) * k] for i in range(3) for j in range(i + 1)]


def dot(left, right, dims=((1,), (0,))):
    return lax.dot_general(
        left, right, (dims, ((), ())),
        precision=lax.Precision.HIGHEST, preferred_element_type=jnp.float32,
    )


NT = ((1,), (1,))
TN = ((0,), (0,))


def split(x):
    high = x.astype(jnp.bfloat16)
    return high, (x - high.astype(jnp.float32)).astype(jnp.bfloat16)


def dot3(left, right):
    def one(a, b):
        return jnp.dot(a, b, preferred_element_type=jnp.float32)

    return one(left[0], right[1]) + one(left[1], right[0]) + one(left[0], right[0])


def inverse_factor(block):
    k = block.shape[0]
    height = 8
    diag = lax.broadcasted_iota(jnp.int32, (k, k), 0) == lax.broadcasted_iota(jnp.int32, (k, k), 1)
    wide = jnp.concatenate([block, diag.astype(jnp.float32)], 1)
    strips = [wide[i : i + height] for i in range(0, k, height)]
    below = lax.broadcasted_iota(jnp.int32, (height, 1), 0)
    for j in range(k):
        at, line = divmod(j, height)
        row = strips[at][line : line + 1]
        row = row * (1.0 / row[:, j : j + 1])
        for i in range(at, k // height):
            col = strips[i][:, j : j + 1]
            if i == at:
                col = jnp.where(below > line, col, 0.0)
            strips[i] = strips[i] - col * row
    wide = jnp.concatenate(strips, 0)
    pivots = jnp.sum(jnp.where(diag, wide[:, :k], 0.0), 1, keepdims=True)
    return wide[:, k:] * (1.0 / jnp.sqrt(pivots))


def ritz_step(k, order, blocks_b, whole_a, inv_ref):
    b00, b10, b11, b20, b21, b22 = blocks_b
    t0 = inverse_factor(b00)
    l10 = dot(b10, t0, NT)
    l20 = dot(b20, t0, NT)
    t1 = inverse_factor(b11 - dot(l10, l10, NT))
    l21 = dot(b21 - dot(l20, l10, NT), t1, NT)
    t2 = inverse_factor(b22 - dot(l20, l20, NT) - dot(l21, l21, NT))
    t10 = -dot(t1, dot(l10, t0))
    t20 = -dot(t2, dot(l20, t0) + dot(l21, t10))
    t21 = -dot(t2, dot(l21, t1))
    inv_ref[...] = jnp.zeros_like(inv_ref)
    inv_ref[:k, :k] = t0
    inv_ref[k : 2 * k, :k] = t10
    inv_ref[k : 2 * k, k : 2 * k] = t1
    inv_ref[2 * k :, : 2 * k] = jnp.concatenate([t20, t21], 1)
    inv_ref[2 * k :, 2 * k :] = t2
    inverse = inv_ref[...]
    middle = dot(dot(inverse, whole_a), inverse, NT)
    middle = 0.5 * (middle + middle.T)
    size = 3 * k
    diag = lax.broadcasted_iota(jnp.int32, (size, size), 0) == lax.broadcasted_iota(
        jnp.int32, (size, size), 1
    )

    def total(x):
        return jnp.sum(jnp.sum(x, 0, keepdims=True), 1, keepdims=True)

    shift = total(jnp.where(diag, middle, 0.0)) * (1.0 / size)
    sign = middle - jnp.where(diag, shift, 0.0)
    sign = sign * (1.0 / jnp.sqrt(total(sign * sign) + 1e-06))
    for turn in range(NS_STEPS):
        parts = split(sign)
        sign = 1.5 * sign - 0.5 * dot3(parts, split(dot3(parts, parts)))
    filtered = 0.5 * (jnp.where(diag, 1.0, 0.0) - sign)[:, :k]
    coords = dot(inverse, filtered, TN) * math.sqrt(order)
    reduced = dot(filtered, dot(middle, filtered), TN)
    return coords, reduced


def put_whole(ref, blocks, k):
    b00, b10, b11, b20, b21, b22 = blocks
    ref[:k, : 2 * k] = jnp.concatenate([b00, b10.T], 1)
    ref[:k, 2 * k :] = b20.T
    ref[k : 2 * k, : 2 * k] = jnp.concatenate([b10, b11], 1)
    ref[k : 2 * k, 2 * k :] = b21.T
    ref[2 * k :, : 2 * k] = jnp.concatenate([b20, b21], 1)
    ref[2 * k :, 2 * k :] = b22
    return ref[...]


def first_kernel(k, order, packed_ref, turn_ref, basis_ref, old_ref, inv_ref, a_ref, b_ref):
    blocks = [packed_ref[i * k : (i + 1) * k] for i in range(6)]
    blocks_a = [x[:, :k] for x in blocks]
    blocks_b = [x[:, k:] for x in blocks]
    whole_a = put_whole(a_ref, blocks_a, k)
    whole_b = put_whole(b_ref, blocks_b, k)
    coords, reduced = ritz_step(k, order, blocks_b, whole_a, inv_ref)
    turn_ref[: 3 * k] = coords
    turn_ref[3 * k :] = -dot(coords, reduced)
    basis_ref[:k] = jnp.concatenate([coords[:k], jnp.zeros((k, k), jnp.float32)], 1)
    basis_ref[k:] = jnp.concatenate([coords[k:], coords[k:]], 1)
    basis = basis_ref[...]
    old_ref[: 2 * k] = dot(basis, dot(whole_a, basis), TN)
    old_ref[2 * k :] = dot(basis, dot(whole_b, basis), TN)


def second_kernel(
    k,
    order,
    old_ref,
    fresh_ref,
    basis_ref,
    own_ref,
    resid_ref,
    prod_ref,
    more_ref,
    out_ref,
    inv_ref,
    a_ref,
):
    def blocks(old, new):
        mid = new[k : 2 * k]
        return [
            old[:k, :k],
            new[:k].T,
            0.5 * (mid + mid.T),
            old[k:, :k],
            new[2 * k :],
            old[k:, k:],
        ]

    whole_a = put_whole(a_ref, blocks(old_ref[: 2 * k], fresh_ref[:, :k]), k)
    blocks_b = blocks(old_ref[2 * k :], fresh_ref[:, k:])
    coords, reduced = ritz_step(k, order, blocks_b, whole_a, inv_ref)
    basis = basis_ref[...]
    from_r = coords[k : 2 * k]
    move_p = dot(basis[:, k:], coords[2 * k :])
    move_x = dot(basis, jnp.concatenate([coords[:k], coords[2 * k :]], 0))
    vectors = jnp.concatenate([own_ref[...], resid_ref[...]], 0)
    out_ref[:k] = dot(jnp.concatenate([move_x, from_r], 0), vectors, TN)
    out_ref[2 * k :] = dot(jnp.concatenate([move_p, from_r], 0), vectors, TN)
    out_ref[k : 2 * k] = (
        dot(move_x, prod_ref[: 3 * k], TN)
        - dot(dot(move_x, reduced), prod_ref[3 * k :], TN)
        + dot(from_r, more_ref[:k], TN)
        - dot(dot(from_r, reduced), more_ref[k:], TN)
    )


def f32(*shape):
    return jax.ShapeDtypeStruct(shape, jnp.float32)


def call(kernel, name, out_shape, scratch, *args):
    return pl.pallas_call(
        kernel,
        out_shape=out_shape,
        scratch_shapes=[pltpu.VMEM(shape, jnp.float32) for shape in scratch],
        compiler_params=pltpu.CompilerParams(vmem_limit_bytes=32 * 2**20),
        name=name,
    )(*args)


def symmetric(x):
    return 0.5 * (x + x.T)


def local(a_matrix, b_matrix, x_block, r_block, p_block):
    rows, cols = lax.axis_size("row"), lax.axis_size("col")
    count = rows * cols
    k = x_block.shape[1]
    order = x_block.shape[0] * rows
    piece = order // count
    high = lax.Precision.HIGH
    to_col = [(b, (b % rows) * cols + b // rows) for b in range(count)]
    to_row = [(d, s) for s, d in to_col]

    panel = jnp.concatenate([x_block.T, r_block.T, p_block.T], 0)
    start = lax.axis_index("col") * piece
    own_row = lax.dynamic_slice_in_dim(panel, start, piece, 1)
    own_col = lax.ppermute(own_row, BOTH, to_col)

    prods = jnp.concatenate(
        [mm(panel, a_matrix, precision=high), mm(panel, b_matrix, precision=high)], 0
    )
    prods_by_piece = prods.reshape(6 * k, rows, piece).transpose(1, 0, 2)
    prod_col = lax.psum_scatter(prods_by_piece, "row", scatter_dimension=0)
    prod_row = lax.ppermute(prod_col, BOTH, to_row)
    matched = share(own_col, "row").transpose(1, 0, 2).reshape(3 * k, -1)
    grams = mm(prods, matched, ((1,), (1,)), high)
    packed = jnp.concatenate(
        [
            jnp.concatenate([ga, gb], 1)
            for ga, gb in zip(
                sides(symmetric(grams[: 3 * k]), k), sides(symmetric(grams[3 * k :]), k)
            )
        ],
        0,
    )
    packed = sum_everywhere(packed)
    turn, basis, old = call(
        functools.partial(first_kernel, k, order),
        "ritz_first",
        (f32(6 * k, k), f32(3 * k, 2 * k), f32(4 * k, 2 * k)),
        [(3 * k, 3 * k)] * 3,
        packed,
    )

    resid_col = mm(turn, prod_col, TN)
    resid_row = mm(turn, prod_row, TN)
    resid = share(resid_col, "row").transpose(1, 0, 2).reshape(k, -1)
    parts = jnp.concatenate(
        [mm(resid, a_matrix, NT, high), mm(resid, b_matrix, NT, high)], 0
    )
    parts = parts.reshape(2 * k, cols, piece).transpose(1, 0, 2)
    more_row = lax.all_to_all(parts, "col", 0, 0).sum(0)

    kept = mm(basis, own_row, TN)
    tests = jnp.concatenate([kept[:k], resid_row, kept[k:]], 0)
    fresh = sum_everywhere(mm(tests, more_row, NT))
    outs = call(
        functools.partial(second_kernel, k, order),
        "ritz_second",
        f32(3 * k, piece),
        [(3 * k, 3 * k)] * 2,
        old,
        fresh,
        basis,
        own_row,
        resid_row,
        prod_row,
        more_row,
    )
    outs = share(outs, "col").transpose(1, 0, 2).reshape(3 * k, -1)
    return (outs[:k].T, outs[k : 2 * k].T, outs[2 * k :].T)


def solution(mesh):
    return jax.shard_map(
        local,
        mesh=mesh,
        in_specs=(P("row", "col"), P("row", "col"), P("row", None), P("row", None), P("row", None)),
        out_specs=(P("row", None), P("row", None), P("row", None)),
        check_vma=False,
    )
```

```python
import functools
import math

import jax
import jax.numpy as jnp
from jax import lax
from jax.experimental import pallas as pl
from jax.experimental.pallas import tpu as pltpu
from jax.sharding import PartitionSpec as P

NS_STEPS = 8
BOTH = ("row", "col")


def mm(left, right, dims=((1,), (0,)), precision=lax.Precision.HIGHEST):
    return lax.dot_general(
        left, right, (dims, ((), ())), precision=precision, preferred_element_type=jnp.float32
    )


def share(x, axis):
    copies = jnp.broadcast_to(x[None], (lax.axis_size(axis),) + x.shape)
    return lax.all_to_all(copies, axis, 0, 0)


def sum_everywhere(x):
    parts = x.reshape(lax.axis_size("row"), -1, x.shape[-1])
    own = lax.all_to_all(parts, "row", 0, 0).sum(0)
    own = share(own, "col").sum(0)
    return share(own, "row").reshape(x.shape)


def dot(left, right, dims=((1,), (0,))):
    return lax.dot_general(
        left, right, (dims, ((), ())),
        precision=lax.Precision.HIGHEST, preferred_element_type=jnp.float32,
    )


NT = ((1,), (1,))
TN = ((0,), (0,))


def split(x):
    high = x.astype(jnp.bfloat16)
    return high, (x - high.astype(jnp.float32)).astype(jnp.bfloat16)


def dot3(left, right):
    def one(a, b):
        return jnp.dot(a, b, preferred_element_type=jnp.float32)

    return one(left[0], right[1]) + one(left[1], right[0]) + one(left[0], right[0])


def inverse_factor(block):
    k = block.shape[0]
    height = 8
    diag = lax.broadcasted_iota(jnp.int32, (k, k), 0) == lax.broadcasted_iota(jnp.int32, (k, k), 1)
    wide = jnp.concatenate([block, diag.astype(jnp.float32)], 1)
    full = (height, 2 * k)
    strips = [wide[i : i + height] for i in range(0, k, height)]
    line = lax.broadcasted_iota(jnp.int32, full, 0)
    done = []
    for at in range(k // height):
        first = at * height
        rows = [jnp.broadcast_to(strips[at][i : i + 1], full) for i in range(height)]
        elem = [
            [jnp.broadcast_to(rows[m][:, first + i : first + i + 1], full) for i in range(m + 1)]
            for m in range(height)
        ]
        later = range(at + 1, k // height)
        cols = {
            t: [
                jnp.broadcast_to(strips[t][:, first + i : first + i + 1], full)
                for i in range(height)
            ]
            for t in later
        }
        low = [[None] * height for _ in range(height)]
        inv = [None] * height
        for i in range(height):
            inv[i] = 1.0 / elem[i][i]
            for m in range(i + 1, height):
                low[m][i] = elem[m][i] * inv[i]
                for n in range(i + 1, m + 1):
                    elem[m][n] = elem[m][n] - low[m][i] * elem[n][i]
                rows[m] = rows[m] - low[m][i] * rows[i]
        out = rows[0] * (1.0 / jnp.sqrt(elem[0][0]))
        for m in range(1, height):
            out = jnp.where(line == m, rows[m] * (1.0 / jnp.sqrt(elem[m][m])), out)
        done.append(out)
        if not later:
            break
        solved = [None] * height
        for m in reversed(range(height)):
            solved[m] = rows[m] * inv[m]
            for i in range(m + 1, height):
                solved[m] = solved[m] - low[i][m] * solved[i]
        for t in later:
            for m in range(height):
                strips[t] = strips[t] - cols[t][m] * solved[m]
    return jnp.concatenate(done, 0)[:, k:]


def ritz_step(k, order, blocks_b, whole_a, inv_ref):
    b00, b10, b11, b20, b21, b22 = blocks_b
    t0 = inverse_factor(b00)
    l10 = dot(b10, t0, NT)
    l20 = dot(b20, t0, NT)
    t1 = inverse_factor(b11 - dot(l10, l10, NT))
    l21 = dot(b21 - dot(l20, l10, NT), t1, NT)
    t2 = inverse_factor(b22 - dot(l20, l20, NT) - dot(l21, l21, NT))
    t10 = -dot(t1, dot(l10, t0))
    t20 = -dot(t2, dot(l20, t0) + dot(l21, t10))
    t21 = -dot(t2, dot(l21, t1))
    inv_ref[...] = jnp.zeros_like(inv_ref)
    inv_ref[:k, :k] = t0
    inv_ref[k : 2 * k, :k] = t10
    inv_ref[k : 2 * k, k : 2 * k] = t1
    inv_ref[2 * k :, : 2 * k] = jnp.concatenate([t20, t21], 1)
    inv_ref[2 * k :, 2 * k :] = t2
    inverse = inv_ref[...]
    middle = dot(dot(inverse, whole_a), inverse, NT)
    middle = 0.5 * (middle + middle.T)
    size = 3 * k
    diag = lax.broadcasted_iota(jnp.int32, (size, size), 0) == lax.broadcasted_iota(
        jnp.int32, (size, size), 1
    )

    def total(x):
        return jnp.sum(jnp.sum(x, 0, keepdims=True), 1, keepdims=True)

    shift = total(jnp.where(diag, middle, 0.0)) * (1.0 / size)
    sign = middle - jnp.where(diag, shift, 0.0)
    sign = sign * (1.0 / jnp.sqrt(total(sign * sign) + 1e-06))
    for turn in range(NS_STEPS):
        parts = split(sign)
        sign = 1.5 * sign - 0.5 * dot3(parts, split(dot3(parts, parts)))
    filtered = 0.5 * (jnp.where(diag, 1.0, 0.0) - sign)[:, :k]
    coords = dot(inverse, filtered, TN) * math.sqrt(order)
    reduced = dot(filtered, dot(middle, filtered), TN)
    return coords, reduced


def put_whole(ref, blocks, k):
    b00, b10, b11, b20, b21, b22 = blocks
    ref[:k, : 2 * k] = jnp.concatenate([b00, b10.T], 1)
    ref[:k, 2 * k :] = b20.T
    ref[k : 2 * k, : 2 * k] = jnp.concatenate([b10, b11], 1)
    ref[k : 2 * k, 2 * k :] = b21.T
    ref[2 * k :, : 2 * k] = jnp.concatenate([b20, b21], 1)
    ref[2 * k :, 2 * k :] = b22
    return ref[...]


def first_kernel(k, order, packed_ref, turn_ref, basis_ref, old_ref, inv_ref, a_ref, b_ref):
    blocks = [packed_ref[i * k : (i + 1) * k] for i in range(6)]
    blocks_a = [x[:, :k] for x in blocks]
    blocks_b = [x[:, k:] for x in blocks]
    whole_a = put_whole(a_ref, blocks_a, k)
    whole_b = put_whole(b_ref, blocks_b, k)
    coords, reduced = ritz_step(k, order, blocks_b, whole_a, inv_ref)
    turn_ref[: 3 * k] = coords
    turn_ref[3 * k :] = -dot(coords, reduced)
    basis_ref[:k] = jnp.concatenate([coords[:k], jnp.zeros((k, k), jnp.float32)], 1)
    basis_ref[k:] = jnp.concatenate([coords[k:], coords[k:]], 1)
    basis = basis_ref[...]
    old_ref[: 2 * k] = dot(basis, dot(whole_a, basis), TN)
    old_ref[2 * k :] = dot(basis, dot(whole_b, basis), TN)


def second_kernel(
    k,
    order,
    old_ref,
    fresh_ref,
    basis_ref,
    own_ref,
    resid_ref,
    prod_ref,
    more_ref,
    out_ref,
    inv_ref,
    a_ref,
):
    def blocks(old, new):
        mid = new[k : 2 * k]
        return [
            old[:k, :k],
            new[:k].T,
            0.5 * (mid + mid.T),
            old[k:, :k],
            new[2 * k :],
            old[k:, k:],
        ]

    whole_a = put_whole(a_ref, blocks(old_ref[: 2 * k], fresh_ref[:, :k]), k)
    blocks_b = blocks(old_ref[2 * k :], fresh_ref[:, k:])
    coords, reduced = ritz_step(k, order, blocks_b, whole_a, inv_ref)
    basis = basis_ref[...]
    from_r = coords[k : 2 * k]
    move_p = dot(basis[:, k:], coords[2 * k :])
    move_x = dot(basis, jnp.concatenate([coords[:k], coords[2 * k :]], 0))
    vectors = jnp.concatenate([own_ref[...], resid_ref[...]], 0)
    out_ref[:k] = dot(jnp.concatenate([move_x, from_r], 0), vectors, TN)
    out_ref[2 * k :] = dot(jnp.concatenate([move_p, from_r], 0), vectors, TN)
    more = more_ref[...].T
    out_ref[k : 2 * k] = (
        dot(move_x, prod_ref[: 3 * k], TN)
        - dot(dot(move_x, reduced), prod_ref[3 * k :], TN)
        + dot(from_r, more[:k], TN)
        - dot(dot(from_r, reduced), more[k:], TN)
    )


def f32(*shape):
    return jax.ShapeDtypeStruct(shape, jnp.float32)


def call(kernel, name, out_shape, scratch, *args):
    return pl.pallas_call(
        kernel,
        out_shape=out_shape,
        scratch_shapes=[pltpu.VMEM(shape, jnp.float32) for shape in scratch],
        compiler_params=pltpu.CompilerParams(vmem_limit_bytes=32 * 2**20),
        name=name,
    )(*args)


def three(left, right, dims):
    def one(a, b):
        return lax.dot_general(a, b, (dims, ((), ())), preferred_element_type=jnp.float32)

    return one(left[0], right[1]) + one(left[1], right[0]) + one(left[0], right[0])


def products_kernel(x_ref, r_ref, p_ref, a_ref, b_ref, out_ref, panel_ref):
    k = x_ref.shape[0]
    wide = 3 * k

    @pl.when(pl.program_id(0) == 0)
    def _():
        for i, ref in enumerate((x_ref, r_ref, p_ref)):
            high, low = split(ref[...])
            panel_ref[i * k : (i + 1) * k] = high
            panel_ref[wide + i * k : wide + (i + 1) * k] = low

    def one(a, b):
        return jnp.dot(a, b, preferred_element_type=jnp.float32)

    for at, ref in ((0, a_ref), (wide, b_ref)):
        high, low = split(ref[...])
        both = one(panel_ref[...], high)
        prod = both[:wide] + both[wide:] + one(panel_ref[:wide], low)
        for i in range(out_ref.shape[0]):
            lanes = out_ref.shape[2]
            out_ref[i, at : at + wide] = prod[:, i * lanes : (i + 1) * lanes]


def gram_kernel(prods_ref, panel_ref, out_ref):
    pieces, wide, lanes = panel_ref.shape
    k = wide // 3
    gram = jnp.zeros((2 * wide, wide), jnp.float32)
    for i in range(0, pieces, 2):
        left = jnp.concatenate([prods_ref[i], prods_ref[i + 1]], 1)
        right = jnp.concatenate([panel_ref[i], panel_ref[i + 1]], 1)
        gram = gram + three(split(left), split(right), NT)
    at = 0
    for i in range(3):
        for j in range(i + 1):
            pair = []
            for base in (0, wide):
                block = gram[base + i * k : base + (i + 1) * k, j * k : (j + 1) * k]
                other = gram[base + j * k : base + (j + 1) * k, i * k : (i + 1) * k]
                pair.append(0.5 * (block + other.T))
            out_ref[at : at + k] = jnp.concatenate(pair, 1)
            at += k


def residual_kernel(resid_ref, a_ref, b_ref, out_ref, first_ref, second_ref):
    pieces, k, lanes = resid_ref.shape

    @pl.when(pl.program_id(0) == 0)
    def _():
        for i in range(pieces):
            block = resid_ref[i].T
            high = block.astype(jnp.bfloat16).astype(jnp.float32)
            low = block - high
            rows = pl.ds(i * lanes, lanes)
            first_ref[rows, :] = jnp.concatenate([high, low], 1).astype(jnp.bfloat16)
            second_ref[rows, :] = jnp.concatenate([low, high], 1).astype(jnp.bfloat16)

    sums = []
    for ref, parts_ref in ((a_ref, first_ref), (b_ref, second_ref)):
        high, low = split(ref[...])
        part = jnp.dot(high, parts_ref[...], preferred_element_type=jnp.float32) + jnp.dot(
            low, parts_ref[...], preferred_element_type=jnp.float32
        )
        sums.append(part + pltpu.roll(part, k, 1))
    lane = lax.broadcasted_iota(jnp.int32, sums[0].shape, 1)
    out_ref[...] = jnp.where(lane < k, sums[0], sums[1])


def products(x, r, p, a, b, pieces):
    k, rows = x.shape
    lanes = a.shape[1] // pieces
    each = 2
    block = pl.BlockSpec((k, rows), lambda i: (0, 0))
    tile = pl.BlockSpec((rows, each * lanes), lambda i: (0, i))
    return pl.pallas_call(
        products_kernel,
        grid=(pieces // each,),
        in_specs=[block, block, block, tile, tile],
        out_specs=pl.BlockSpec((each, 6 * k, lanes), lambda i: (i, 0, 0)),
        out_shape=f32(pieces, 6 * k, lanes),
        scratch_shapes=[pltpu.VMEM((6 * k, rows), jnp.bfloat16)],
        compiler_params=pltpu.CompilerParams(vmem_limit_bytes=48 * 2**20),
        name="products",
    )(x, r, p, a, b)


def residual_products(resid, a, b):
    pieces, k, lanes = resid.shape
    rows, cols = a.shape
    height = 512
    tile = pl.BlockSpec((height, cols), lambda i: (i, 0))
    return pl.pallas_call(
        residual_kernel,
        grid=(rows // height,),
        in_specs=[pl.BlockSpec(resid.shape, lambda i: (0, 0, 0)), tile, tile],
        out_specs=pl.BlockSpec((height, 2 * k), lambda i: (i, 0)),
        out_shape=f32(rows, 2 * k),
        scratch_shapes=[pltpu.VMEM((cols, 2 * k), jnp.bfloat16)] * 2,
        compiler_params=pltpu.CompilerParams(vmem_limit_bytes=48 * 2**20),
        name="residual_products",
    )(resid, a, b)


def local(a_matrix, b_matrix, x_block, r_block, p_block):
    rows, cols = lax.axis_size("row"), lax.axis_size("col")
    count = rows * cols
    k = x_block.shape[1]
    order = x_block.shape[0] * rows
    piece = order // count
    to_col = [(b, (b % rows) * cols + b // rows) for b in range(count)]
    to_row = [(d, s) for s, d in to_col]

    panel = [x_block.T, r_block.T, p_block.T]
    start = lax.axis_index("col") * piece
    own_row = jnp.concatenate(
        [lax.dynamic_slice_in_dim(x, start, piece, 1) for x in panel], 0
    )
    own_col = lax.ppermute(own_row, BOTH, to_col)

    prods = products(*panel, a_matrix, b_matrix, rows)
    prod_col = lax.psum_scatter(prods, "row", scatter_dimension=0)
    prod_row = lax.ppermute(prod_col, BOTH, to_row)
    matched = share(own_col, "row")
    packed = sum_everywhere(call(gram_kernel, "gram", f32(6 * k, 2 * k), [], prods, matched))
    packed, prod_row = lax.optimization_barrier((packed, prod_row))
    turn, basis, old = call(
        functools.partial(first_kernel, k, order),
        "ritz_first",
        (f32(6 * k, k), f32(3 * k, 2 * k), f32(4 * k, 2 * k)),
        [(3 * k, 3 * k)] * 3,
        packed,
    )

    resid_col = mm(turn, prod_col, TN)
    resid_row = mm(turn, prod_row, TN)
    parts = residual_products(share(resid_col, "row"), a_matrix, b_matrix)
    parts = parts.reshape(cols, piece, 2 * k)
    more_row = lax.all_to_all(parts, "col", 0, 0).sum(0)

    kept = mm(basis, own_row, TN)
    tests = jnp.concatenate([kept[:k], resid_row, kept[k:]], 0)
    fresh = sum_everywhere(mm(tests, more_row))
    outs = call(
        functools.partial(second_kernel, k, order),
        "ritz_second",
        f32(3 * k, piece),
        [(3 * k, 3 * k)] * 2,
        old,
        fresh,
        basis,
        own_row,
        resid_row,
        prod_row,
        more_row,
    )
    outs = share(outs, "col").transpose(1, 0, 2).reshape(3 * k, -1)
    return (outs[:k].T, outs[k : 2 * k].T, outs[2 * k :].T)


def solution(mesh):
    return jax.shard_map(
        local,
        mesh=mesh,
        in_specs=(P("row", "col"), P("row", "col"), P("row", None), P("row", None), P("row", None)),
        out_specs=(P("row", None), P("row", None), P("row", None)),
        check_vma=False,
    )
```

```python
import functools
import math

import jax
import jax.numpy as jnp
from jax import lax
from jax.experimental import pallas as pl
from jax.experimental.pallas import tpu as pltpu
from jax.sharding import PartitionSpec as P

NS_STEPS = 8
BOTH = ("row", "col")


def mm(left, right, dims=((1,), (0,)), precision=lax.Precision.HIGHEST):
    return lax.dot_general(
        left, right, (dims, ((), ())), precision=precision, preferred_element_type=jnp.float32
    )


def share(x, axis):
    copies = jnp.broadcast_to(x[None], (lax.axis_size(axis),) + x.shape)
    return lax.all_to_all(copies, axis, 0, 0)


def sum_everywhere(x):
    parts = x.reshape(lax.axis_size("row"), -1, x.shape[-1])
    own = lax.all_to_all(parts, "row", 0, 0).sum(0)
    own = share(own, "col").sum(0)
    return share(own, "row").reshape(x.shape)


def dot(left, right, dims=((1,), (0,))):
    return lax.dot_general(
        left, right, (dims, ((), ())),
        precision=lax.Precision.HIGHEST, preferred_element_type=jnp.float32,
    )


NT = ((1,), (1,))
TN = ((0,), (0,))


def split(x):
    high = x.astype(jnp.bfloat16)
    return high, (x - high.astype(jnp.float32)).astype(jnp.bfloat16)


def dot3(left, right):
    def one(a, b):
        return jnp.dot(a, b, preferred_element_type=jnp.float32)

    return one(left[0], right[1]) + one(left[1], right[0]) + one(left[0], right[0])


def inverse_factor(block):
    k = block.shape[0]
    height = 8
    diag = lax.broadcasted_iota(jnp.int32, (k, k), 0) == lax.broadcasted_iota(jnp.int32, (k, k), 1)
    wide = jnp.concatenate([block, diag.astype(jnp.float32)], 1)
    full = (height, 2 * k)
    strips = [wide[i : i + height] for i in range(0, k, height)]
    line = lax.broadcasted_iota(jnp.int32, full, 0)
    done = []
    for at in range(k // height):
        first = at * height
        rows = [jnp.broadcast_to(strips[at][i : i + 1], full) for i in range(height)]
        elem = [
            [jnp.broadcast_to(rows[m][:, first + i : first + i + 1], full) for i in range(m + 1)]
            for m in range(height)
        ]
        later = range(at + 1, k // height)
        cols = {
            t: [
                jnp.broadcast_to(strips[t][:, first + i : first + i + 1], full)
                for i in range(height)
            ]
            for t in later
        }
        low = [[None] * height for _ in range(height)]
        inv = [None] * height
        for i in range(height):
            inv[i] = 1.0 / elem[i][i]
            for m in range(i + 1, height):
                low[m][i] = elem[m][i] * inv[i]
                for n in range(i + 1, m + 1):
                    elem[m][n] = elem[m][n] - low[m][i] * elem[n][i]
                rows[m] = rows[m] - low[m][i] * rows[i]
        out = rows[0] * (1.0 / jnp.sqrt(elem[0][0]))
        for m in range(1, height):
            out = jnp.where(line == m, rows[m] * (1.0 / jnp.sqrt(elem[m][m])), out)
        done.append(out)
        if not later:
            break
        solved = [None] * height
        for m in reversed(range(height)):
            solved[m] = rows[m] * inv[m]
            for i in range(m + 1, height):
                solved[m] = solved[m] - low[i][m] * solved[i]
        for t in later:
            for m in range(height):
                strips[t] = strips[t] - cols[t][m] * solved[m]
    return jnp.concatenate(done, 0)[:, k:]


def ritz_step(k, order, blocks_b, whole_a, inv_ref):
    b00, b10, b11, b20, b21, b22 = blocks_b
    t0 = inverse_factor(b00)
    l10 = dot(b10, t0, NT)
    l20 = dot(b20, t0, NT)
    t1 = inverse_factor(b11 - dot(l10, l10, NT))
    l21 = dot(b21 - dot(l20, l10, NT), t1, NT)
    t2 = inverse_factor(b22 - dot(l20, l20, NT) - dot(l21, l21, NT))
    t10 = -dot(t1, dot(l10, t0))
    t20 = -dot(t2, dot(l20, t0) + dot(l21, t10))
    t21 = -dot(t2, dot(l21, t1))
    inv_ref[...] = jnp.zeros_like(inv_ref)
    inv_ref[:k, :k] = t0
    inv_ref[k : 2 * k, :k] = t10
    inv_ref[k : 2 * k, k : 2 * k] = t1
    inv_ref[2 * k :, : 2 * k] = jnp.concatenate([t20, t21], 1)
    inv_ref[2 * k :, 2 * k :] = t2
    inverse = inv_ref[...]
    middle = dot(dot(inverse, whole_a), inverse, NT)
    middle = 0.5 * (middle + middle.T)
    size = 3 * k
    diag = lax.broadcasted_iota(jnp.int32, (size, size), 0) == lax.broadcasted_iota(
        jnp.int32, (size, size), 1
    )

    def total(x):
        return jnp.sum(jnp.sum(x, 0, keepdims=True), 1, keepdims=True)

    shift = total(jnp.where(diag, middle, 0.0)) * (1.0 / size)
    sign = middle - jnp.where(diag, shift, 0.0)
    sign = sign * (1.0 / jnp.sqrt(total(sign * sign) + 1e-06))
    for turn in range(NS_STEPS):
        parts = split(sign)
        sign = 1.5 * sign - 0.5 * dot3(parts, split(dot3(parts, parts)))
    filtered = 0.5 * (jnp.where(diag, 1.0, 0.0) - sign)[:, :k]
    coords = dot(inverse, filtered, TN) * math.sqrt(order)
    reduced = dot(filtered, dot(middle, filtered), TN)
    return coords, reduced


def put_whole(ref, blocks, k):
    b00, b10, b11, b20, b21, b22 = blocks
    ref[:k, : 2 * k] = jnp.concatenate([b00, b10.T], 1)
    ref[:k, 2 * k :] = b20.T
    ref[k : 2 * k, : 2 * k] = jnp.concatenate([b10, b11], 1)
    ref[k : 2 * k, 2 * k :] = b21.T
    ref[2 * k :, : 2 * k] = jnp.concatenate([b20, b21], 1)
    ref[2 * k :, 2 * k :] = b22
    return ref[...]


def first_kernel(k, order, packed_ref, turn_ref, basis_ref, old_ref, inv_ref, a_ref, b_ref):
    blocks = [packed_ref[i * k : (i + 1) * k] for i in range(6)]
    blocks_a = [x[:, :k] for x in blocks]
    blocks_b = [x[:, k:] for x in blocks]
    whole_a = put_whole(a_ref, blocks_a, k)
    whole_b = put_whole(b_ref, blocks_b, k)
    coords, reduced = ritz_step(k, order, blocks_b, whole_a, inv_ref)
    turn_ref[: 3 * k] = coords
    turn_ref[3 * k :] = -dot(coords, reduced)
    basis_ref[:k] = jnp.concatenate([coords[:k], jnp.zeros((k, k), jnp.float32)], 1)
    basis_ref[k:] = jnp.concatenate([coords[k:], coords[k:]], 1)
    basis = basis_ref[...]
    old_ref[: 2 * k] = dot(basis, dot(whole_a, basis), TN)
    old_ref[2 * k :] = dot(basis, dot(whole_b, basis), TN)


def second_kernel(
    k,
    order,
    old_ref,
    fresh_ref,
    basis_ref,
    turn_ref,
    prod_ref,
    more_ref,
    r_ref,
    mix_ref,
    inv_ref,
    a_ref,
):
    def blocks(old, new):
        mid = new[k : 2 * k]
        return [
            old[:k, :k],
            new[:k].T,
            0.5 * (mid + mid.T),
            old[k:, :k],
            new[2 * k :],
            old[k:, k:],
        ]

    whole_a = put_whole(a_ref, blocks(old_ref[: 2 * k], fresh_ref[:, :k]), k)
    blocks_b = blocks(old_ref[2 * k :], fresh_ref[:, k:])
    coords, reduced = ritz_step(k, order, blocks_b, whole_a, inv_ref)
    basis = basis_ref[...]
    from_r = coords[k : 2 * k]
    move_p = dot(basis[:, k:], coords[2 * k :])
    move_x = dot(basis, jnp.concatenate([coords[:k], coords[2 * k :]], 0))
    more = more_ref[...].T
    shared = dot(turn_ref[...], from_r)
    mix_ref[: 3 * k] = jnp.concatenate([move_x, move_p], 1)
    mix_ref[3 * k :] = jnp.concatenate([shared, shared], 1)
    r_ref[...] = (
        dot(move_x, prod_ref[: 3 * k], TN)
        - dot(dot(move_x, reduced), prod_ref[3 * k :], TN)
        + dot(from_r, more[:k], TN)
        - dot(dot(from_r, reduced), more[k:], TN)
    )


def f32(*shape):
    return jax.ShapeDtypeStruct(shape, jnp.float32)


def cost(flops, size):
    return pl.CostEstimate(flops=int(flops), bytes_accessed=int(size), transcendentals=0)


def call(kernel, name, out_shape, scratch, flops, *args):
    return pl.pallas_call(
        kernel,
        out_shape=out_shape,
        scratch_shapes=[pltpu.VMEM(shape, jnp.float32) for shape in scratch],
        compiler_params=pltpu.CompilerParams(vmem_limit_bytes=32 * 2**20),
        cost_estimate=cost(flops, 2**20),
        name=name,
    )(*args)


def three(left, right, dims):
    def one(a, b):
        return lax.dot_general(a, b, (dims, ((), ())), preferred_element_type=jnp.float32)

    return one(left[0], right[1]) + one(left[1], right[0]) + one(left[0], right[0])


def products_kernel(x_ref, r_ref, p_ref, a_ref, b_ref, out_ref, panel_ref):
    k = x_ref.shape[0]
    wide = 3 * k

    @pl.when(pl.program_id(0) == 0)
    def _():
        for i, ref in enumerate((x_ref, r_ref, p_ref)):
            high, low = split(ref[...])
            panel_ref[i * k : (i + 1) * k] = high
            panel_ref[wide + i * k : wide + (i + 1) * k] = low

    def one(a, b):
        return jnp.dot(a, b, preferred_element_type=jnp.float32)

    for at, ref in ((0, a_ref), (wide, b_ref)):
        high, low = split(ref[...])
        both = one(panel_ref[...], high)
        prod = both[:wide] + both[wide:] + one(panel_ref[:wide], low)
        for i in range(out_ref.shape[0]):
            lanes = out_ref.shape[2]
            out_ref[i, at : at + wide] = prod[:, i * lanes : (i + 1) * lanes]


def gram_kernel(parts_ref, panel_ref, prods_ref, out_ref):
    wide = panel_ref.shape[0]
    k = wide // 3
    prods = parts_ref[0]
    for i in range(1, parts_ref.shape[0]):
        prods = prods + parts_ref[i]
    prods_ref[...] = prods
    gram = three(split(prods), split(panel_ref[...]), NT)
    at = 0
    for i in range(3):
        for j in range(i + 1):
            pair = []
            for base in (0, wide):
                block = gram[base + i * k : base + (i + 1) * k, j * k : (j + 1) * k]
                other = gram[base + j * k : base + (j + 1) * k, i * k : (i + 1) * k]
                pair.append(0.5 * (block + other.T))
            out_ref[at : at + k] = jnp.concatenate(pair, 1)
            at += k


def fresh_kernel(parts_ref, turn_ref, prods_ref, basis_ref, own_ref, more_ref, resid_ref, out_ref):
    k = turn_ref.shape[1]
    more = parts_ref[0]
    for i in range(1, parts_ref.shape[0]):
        more = more + parts_ref[i]
    more_ref[...] = more
    resid = dot(turn_ref[...], prods_ref[...], TN)
    resid_ref[...] = resid
    kept = dot(basis_ref[...], own_ref[...], TN)
    tests = jnp.concatenate([kept[:k], resid, kept[k:]], 0)
    out_ref[...] = three(split(tests), split(more), ((1,), (0,)))


def outputs_kernel(mix_ref, x_ref, r_ref, p_ref, prods_ref, x_out, p_out):
    k = x_ref.shape[0]
    prods = jnp.concatenate([prods_ref[i] for i in range(prods_ref.shape[0])], 1)
    vectors = jnp.concatenate([x_ref[...], r_ref[...], p_ref[...], prods], 0)
    out = three(split(mix_ref[...]), split(vectors), TN)
    x_out[...] = out[:k]
    p_out[...] = out[k:]


def residual_kernel(turn_ref, prods_ref, a_ref, b_ref, out_ref, first_ref, second_ref):
    pieces, _, lanes = prods_ref.shape
    k = turn_ref.shape[1]

    @pl.when(pl.program_id(0) == 0)
    def _():
        turn = split(turn_ref[...])
        for i in range(pieces):
            block = three(split(prods_ref[i]), turn, TN)
            high = block.astype(jnp.bfloat16).astype(jnp.float32)
            low = block - high
            rows = pl.ds(i * lanes, lanes)
            first_ref[rows, :] = jnp.concatenate([high, low], 1).astype(jnp.bfloat16)
            second_ref[rows, :] = jnp.concatenate([low, high], 1).astype(jnp.bfloat16)

    sums = []
    for ref, parts_ref in ((a_ref, first_ref), (b_ref, second_ref)):
        high, low = split(ref[...])
        part = jnp.dot(high, parts_ref[...], preferred_element_type=jnp.float32) + jnp.dot(
            low, parts_ref[...], preferred_element_type=jnp.float32
        )
        sums.append(part + pltpu.roll(part, k, 1))
    lane = lax.broadcasted_iota(jnp.int32, sums[0].shape, 1)
    out_ref[...] = jnp.where(lane < k, sums[0], sums[1])


def products(x, r, p, a, b, pieces):
    k, rows = x.shape
    lanes = a.shape[1] // pieces
    each = 2
    block = pl.BlockSpec((k, rows), lambda i: (0, 0))
    tile = pl.BlockSpec((rows, each * lanes), lambda i: (0, i))
    return pl.pallas_call(
        products_kernel,
        grid=(pieces // each,),
        in_specs=[block, block, block, tile, tile],
        out_specs=pl.BlockSpec((each, 6 * k, lanes), lambda i: (i, 0, 0)),
        out_shape=f32(pieces, 6 * k, lanes),
        scratch_shapes=[pltpu.VMEM((6 * k, rows), jnp.bfloat16)],
        compiler_params=pltpu.CompilerParams(vmem_limit_bytes=60 * 2**20),
        cost_estimate=cost(1e10, 8 * rows * a.shape[1]),
        name="products",
    )(x, r, p, a, b)


def residual_products(turn, prods, a, b):
    k = turn.shape[1]
    rows, cols = a.shape
    height = 512
    tile = pl.BlockSpec((height, cols), lambda i: (i, 0))
    return pl.pallas_call(
        residual_kernel,
        grid=(rows // height,),
        in_specs=[
            pl.BlockSpec(turn.shape, lambda i: (0, 0)),
            pl.BlockSpec(prods.shape, lambda i: (0, 0, 0)),
            tile,
            tile,
        ],
        out_specs=pl.BlockSpec((height, 2 * k), lambda i: (i, 0)),
        out_shape=f32(rows, 2 * k),
        scratch_shapes=[pltpu.VMEM((cols, 2 * k), jnp.bfloat16)] * 2,
        compiler_params=pltpu.CompilerParams(vmem_limit_bytes=60 * 2**20),
        cost_estimate=cost(1e10, 8 * rows * cols),
        name="residual_products",
    )(turn, prods, a, b)


def outputs(mix, x, r, p, prods):
    k, rows = x.shape
    pieces, wide, lanes = prods.shape
    each = 4
    part = pl.BlockSpec((k, each * lanes), lambda i: (0, i))
    return pl.pallas_call(
        outputs_kernel,
        grid=(pieces // each,),
        in_specs=[
            pl.BlockSpec(mix.shape, lambda i: (0, 0)),
            part,
            part,
            part,
            pl.BlockSpec((each, wide, lanes), lambda i: (i, 0, 0)),
        ],
        out_specs=(part, part),
        out_shape=(f32(k, rows), f32(k, rows)),
        compiler_params=pltpu.CompilerParams(vmem_limit_bytes=60 * 2**20),
        cost_estimate=cost(3e9, 12 * rows * wide),
        name="outputs",
    )(mix, x, r, p, prods)


def local(a_matrix, b_matrix, x_block, r_block, p_block):
    rows, cols = lax.axis_size("row"), lax.axis_size("col")
    count = rows * cols
    k = x_block.shape[1]
    order = x_block.shape[0] * rows
    piece = order // count
    to_col = [(b, (b % rows) * cols + b // rows) for b in range(count)]
    to_row = [(d, s) for s, d in to_col]

    panel = [x_block.T, r_block.T, p_block.T]
    start = lax.axis_index("col") * piece
    own_row = jnp.concatenate(
        [lax.dynamic_slice_in_dim(x, start, piece, 1) for x in panel], 0
    )
    own_col = lax.ppermute(own_row, BOTH, to_col)

    prods = products(*panel, a_matrix, b_matrix, rows)
    prods = lax.all_to_all(prods, "row", 0, 0)
    prod_col, packed = call(
        gram_kernel, "gram", (f32(6 * k, piece), f32(6 * k, 2 * k)), [], 2e9, prods, own_col
    )
    prod_row = lax.ppermute(prod_col, BOTH, to_row)
    prods_col = lax.all_gather(prod_col, "row")
    prods_row = lax.all_gather(prod_row, "col")
    packed = sum_everywhere(packed)
    turn, basis, old = call(
        functools.partial(first_kernel, k, order),
        "ritz_first",
        (f32(6 * k, k), f32(3 * k, 2 * k), f32(4 * k, 2 * k)),
        [(3 * k, 3 * k)] * 3,
        1.7e10,
        packed,
    )

    parts = residual_products(turn, prods_col, a_matrix, b_matrix)
    parts = lax.all_to_all(parts.reshape(cols, piece, 2 * k), "col", 0, 0)
    more_row, resid_row, fresh = call(
        fresh_kernel,
        "fresh",
        (f32(piece, 2 * k), f32(k, piece), f32(3 * k, 2 * k)),
        [],
        1e9,
        parts,
        turn,
        prod_row,
        basis,
        own_row,
    )
    fresh = sum_everywhere(fresh)
    r_own, mix = call(
        functools.partial(second_kernel, k, order),
        "ritz_second",
        (f32(k, piece), f32(9 * k, 2 * k)),
        [(3 * k, 3 * k)] * 2,
        1.7e10,
        old,
        fresh,
        basis,
        turn,
        prod_row,
        more_row,
    )
    r_next = share(r_own, "col")
    x_next, p_next = outputs(mix, *panel, prods_row)
    r_next, x_next, p_next = lax.optimization_barrier((r_next, x_next, p_next))
    r_next = r_next.transpose(1, 0, 2).reshape(k, -1)
    return (x_next.T, r_next.T, p_next.T)


def solution(mesh):
    return jax.shard_map(
        local,
        mesh=mesh,
        in_specs=(P("row", "col"), P("row", "col"), P("row", None), P("row", None), P("row", None)),
        out_specs=(P("row", None), P("row", None), P("row", None)),
        check_vma=False,
    )
```

```python
import functools
import math

import jax
import jax.numpy as jnp
from jax import lax
from jax.experimental import pallas as pl
from jax.experimental.pallas import tpu as pltpu
from jax.sharding import PartitionSpec as P

NS_STEPS = 8
BOTH = ("row", "col")


def mm(left, right, dims=((1,), (0,)), precision=lax.Precision.HIGHEST):
    return lax.dot_general(
        left, right, (dims, ((), ())), precision=precision, preferred_element_type=jnp.float32
    )


def share(x, axis):
    copies = jnp.broadcast_to(x[None], (lax.axis_size(axis),) + x.shape)
    return lax.all_to_all(copies, axis, 0, 0)


def sum_everywhere(x):
    parts = x.reshape(lax.axis_size("row"), -1, x.shape[-1])
    own = lax.all_to_all(parts, "row", 0, 0).sum(0)
    own = share(own, "col").sum(0)
    return share(own, "row").reshape(x.shape)


def dot(left, right, dims=((1,), (0,))):
    return lax.dot_general(
        left, right, (dims, ((), ())),
        precision=lax.Precision.HIGHEST, preferred_element_type=jnp.float32,
    )


NT = ((1,), (1,))
TN = ((0,), (0,))


def split(x):
    high = x.astype(jnp.bfloat16)
    return high, (x - high.astype(jnp.float32)).astype(jnp.bfloat16)


def dot3(left, right):
    def one(a, b):
        return jnp.dot(a, b, preferred_element_type=jnp.float32)

    return one(left[0], right[1]) + one(left[1], right[0]) + one(left[0], right[0])


def inverse_factor(block):
    k = block.shape[0]
    height = 8
    diag = lax.broadcasted_iota(jnp.int32, (k, k), 0) == lax.broadcasted_iota(jnp.int32, (k, k), 1)
    wide = jnp.concatenate([block, diag.astype(jnp.float32)], 1)
    full = (height, 2 * k)
    strips = [wide[i : i + height] for i in range(0, k, height)]
    line = lax.broadcasted_iota(jnp.int32, full, 0)
    done = []
    for at in range(k // height):
        first = at * height
        rows = [jnp.broadcast_to(strips[at][i : i + 1], full) for i in range(height)]
        elem = [
            [jnp.broadcast_to(rows[m][:, first + i : first + i + 1], full) for i in range(m + 1)]
            for m in range(height)
        ]
        later = range(at + 1, k // height)
        cols = {
            t: [
                jnp.broadcast_to(strips[t][:, first + i : first + i + 1], full)
                for i in range(height)
            ]
            for t in later
        }
        low = [[None] * height for _ in range(height)]
        inv = {}
        out = None
        for i in range(0, height, 2):
            a, b, c = elem[i][i], elem[i + 1][i], elem[i + 1][i + 1]
            det = a * c - b * b
            inv[i] = 1.0 / det
            for m in range(i + 2, height):
                u, v = elem[m][i], elem[m][i + 1]
                low[m][i] = (u * c - v * b) * inv[i]
                low[m][i + 1] = (v * a - u * b) * inv[i]
                for n in range(i + 2, m + 1):
                    elem[m][n] = elem[m][n] - (
                        low[m][i] * elem[n][i] + low[m][i + 1] * elem[n][i + 1]
                    )
                rows[m] = rows[m] - (low[m][i] * rows[i] + low[m][i + 1] * rows[i + 1])
            scale = 1.0 / a
            upper = rows[i] * (1.0 / jnp.sqrt(a))
            lower = (rows[i + 1] - (b * scale) * rows[i]) * (1.0 / jnp.sqrt(det * scale))
            out = upper if out is None else jnp.where(line == i, upper, out)
            out = jnp.where(line == i + 1, lower, out)
        done.append(out)
        if not later:
            break
        solved = [None] * height
        for i in reversed(range(0, height, 2)):
            a, b, c = elem[i][i], elem[i + 1][i], elem[i + 1][i + 1]
            solved[i] = (c * rows[i] - b * rows[i + 1]) * inv[i]
            solved[i + 1] = (a * rows[i + 1] - b * rows[i]) * inv[i]
            for m in range(i + 2, height):
                solved[i] = solved[i] - low[m][i] * solved[m]
                solved[i + 1] = solved[i + 1] - low[m][i + 1] * solved[m]
        for t in later:
            for m in range(height):
                strips[t] = strips[t] - cols[t][m] * solved[m]
    return jnp.concatenate(done, 0)[:, k:]


def ritz_step(k, order, blocks_b, whole_a, inv_ref):
    b00, b10, b11, b20, b21, b22 = blocks_b
    t0 = inverse_factor(b00)
    l10 = dot(b10, t0, NT)
    l20 = dot(b20, t0, NT)
    t1 = inverse_factor(b11 - dot(l10, l10, NT))
    l21 = dot(b21 - dot(l20, l10, NT), t1, NT)
    t2 = inverse_factor(b22 - dot(l20, l20, NT) - dot(l21, l21, NT))
    t10 = -dot(t1, dot(l10, t0))
    t20 = -dot(t2, dot(l20, t0) + dot(l21, t10))
    t21 = -dot(t2, dot(l21, t1))
    inv_ref[...] = jnp.zeros_like(inv_ref)
    inv_ref[:k, :k] = t0
    inv_ref[k : 2 * k, :k] = t10
    inv_ref[k : 2 * k, k : 2 * k] = t1
    inv_ref[2 * k :, : 2 * k] = jnp.concatenate([t20, t21], 1)
    inv_ref[2 * k :, 2 * k :] = t2
    inverse = inv_ref[...]
    middle = dot(dot(inverse, whole_a), inverse, NT)
    middle = 0.5 * (middle + middle.T)
    size = 3 * k
    diag = lax.broadcasted_iota(jnp.int32, (size, size), 0) == lax.broadcasted_iota(
        jnp.int32, (size, size), 1
    )

    def total(x):
        return jnp.sum(jnp.sum(x, 0, keepdims=True), 1, keepdims=True)

    shift = total(jnp.where(diag, middle, 0.0)) * (1.0 / size)
    sign = middle - jnp.where(diag, shift, 0.0)
    sign = sign * (1.0 / jnp.sqrt(total(sign * sign) + 1e-06))
    for turn in range(NS_STEPS):
        parts = split(sign)
        sign = 1.5 * sign - 0.5 * dot3(parts, split(dot3(parts, parts)))
    filtered = 0.5 * (jnp.where(diag, 1.0, 0.0) - sign)[:, :k]
    coords = dot(inverse, filtered, TN) * math.sqrt(order)
    reduced = dot(filtered, dot(middle, filtered), TN)
    return coords, reduced


def put_whole(ref, blocks, k):
    b00, b10, b11, b20, b21, b22 = blocks
    ref[:k, : 2 * k] = jnp.concatenate([b00, b10.T], 1)
    ref[:k, 2 * k :] = b20.T
    ref[k : 2 * k, : 2 * k] = jnp.concatenate([b10, b11], 1)
    ref[k : 2 * k, 2 * k :] = b21.T
    ref[2 * k :, : 2 * k] = jnp.concatenate([b20, b21], 1)
    ref[2 * k :, 2 * k :] = b22
    return ref[...]


def first_kernel(k, order, packed_ref, turn_ref, basis_ref, old_ref, inv_ref, a_ref, b_ref):
    blocks = [packed_ref[i * k : (i + 1) * k] for i in range(6)]
    blocks_a = [x[:, :k] for x in blocks]
    blocks_b = [x[:, k:] for x in blocks]
    whole_a = put_whole(a_ref, blocks_a, k)
    whole_b = put_whole(b_ref, blocks_b, k)
    coords, reduced = ritz_step(k, order, blocks_b, whole_a, inv_ref)
    turn_ref[: 3 * k] = coords
    turn_ref[3 * k :] = -dot(coords, reduced)
    basis_ref[:k] = jnp.concatenate([coords[:k], jnp.zeros((k, k), jnp.float32)], 1)
    basis_ref[k:] = jnp.concatenate([coords[k:], coords[k:]], 1)
    basis = basis_ref[...]
    old_ref[: 2 * k] = dot(basis, dot(whole_a, basis), TN)
    old_ref[2 * k :] = dot(basis, dot(whole_b, basis), TN)


def second_kernel(
    k,
    order,
    old_ref,
    fresh_ref,
    basis_ref,
    prod_ref,
    more_ref,
    r_ref,
    mix_ref,
    inv_ref,
    a_ref,
):
    def blocks(old, new):
        mid = new[k : 2 * k]
        return [
            old[:k, :k],
            new[:k].T,
            0.5 * (mid + mid.T),
            old[k:, :k],
            new[2 * k :],
            old[k:, k:],
        ]

    whole_a = put_whole(a_ref, blocks(old_ref[: 2 * k], fresh_ref[:, :k]), k)
    blocks_b = blocks(old_ref[2 * k :], fresh_ref[:, k:])
    coords, reduced = ritz_step(k, order, blocks_b, whole_a, inv_ref)
    basis = basis_ref[...]
    from_r = coords[k : 2 * k]
    move_p = dot(basis[:, k:], coords[2 * k :])
    move_x = dot(basis, jnp.concatenate([coords[:k], coords[2 * k :]], 0))
    more = more_ref[...].T
    mix_ref[: 3 * k] = jnp.concatenate([move_x, move_p], 1)
    mix_ref[3 * k :] = jnp.concatenate([from_r, from_r], 1)
    r_ref[...] = (
        dot(move_x, prod_ref[: 3 * k], TN)
        - dot(dot(move_x, reduced), prod_ref[3 * k :], TN)
        + dot(from_r, more[:k], TN)
        - dot(dot(from_r, reduced), more[k:], TN)
    )


def f32(*shape):
    return jax.ShapeDtypeStruct(shape, jnp.float32)


def cost(flops, size):
    return pl.CostEstimate(flops=int(flops), bytes_accessed=int(size), transcendentals=0)


def call(kernel, name, out_shape, scratch, flops, *args):
    return pl.pallas_call(
        kernel,
        out_shape=out_shape,
        scratch_shapes=[pltpu.VMEM(shape, jnp.float32) for shape in scratch],
        compiler_params=pltpu.CompilerParams(vmem_limit_bytes=32 * 2**20),
        cost_estimate=cost(flops, 2**20),
        name=name,
    )(*args)


def three(left, right, dims):
    def one(a, b):
        return lax.dot_general(a, b, (dims, ((), ())), preferred_element_type=jnp.float32)

    return one(left[0], right[1]) + one(left[1], right[0]) + one(left[0], right[0])


def products_kernel(x_ref, r_ref, p_ref, a_ref, b_ref, out_ref, panel_ref):
    k = x_ref.shape[0]
    wide = 3 * k

    @pl.when(pl.program_id(0) == 0)
    def _():
        for i, ref in enumerate((x_ref, r_ref, p_ref)):
            high, low = split(ref[...])
            panel_ref[i * k : (i + 1) * k] = high
            panel_ref[wide + i * k : wide + (i + 1) * k] = low

    def one(a, b):
        return jnp.dot(a, b, preferred_element_type=jnp.float32)

    for at, ref in ((0, a_ref), (wide, b_ref)):
        high, low = split(ref[...])
        both = one(panel_ref[...], high)
        prod = both[:wide] + both[wide:] + one(panel_ref[:wide], low)
        for i in range(out_ref.shape[0]):
            lanes = out_ref.shape[2]
            out_ref[i, at : at + wide] = prod[:, i * lanes : (i + 1) * lanes]


def gram_kernel(parts_ref, panel_ref, prods_ref, out_ref):
    wide = panel_ref.shape[0]
    k = wide // 3
    prods = parts_ref[0]
    for i in range(1, parts_ref.shape[0]):
        prods = prods + parts_ref[i]
    prods_ref[...] = prods
    gram = three(split(prods), split(panel_ref[...]), NT)
    at = 0
    for i in range(3):
        for j in range(i + 1):
            pair = []
            for base in (0, wide):
                block = gram[base + i * k : base + (i + 1) * k, j * k : (j + 1) * k]
                other = gram[base + j * k : base + (j + 1) * k, i * k : (i + 1) * k]
                pair.append(0.5 * (block + other.T))
            out_ref[at : at + k] = jnp.concatenate(pair, 1)
            at += k


def fresh_kernel(parts_ref, turn_ref, prods_ref, basis_ref, own_ref, more_ref, resid_ref, out_ref):
    k = turn_ref.shape[1]
    more = parts_ref[0]
    for i in range(1, parts_ref.shape[0]):
        more = more + parts_ref[i]
    more_ref[...] = more
    resid = dot(turn_ref[...], prods_ref[...], TN)
    resid_ref[:k] = resid
    resid_ref[k:] = jnp.zeros_like(resid)
    kept = dot(basis_ref[...], own_ref[...], TN)
    tests = jnp.concatenate([kept[:k], resid, kept[k:]], 0)
    out_ref[...] = three(split(tests), split(more), ((1,), (0,)))


def outputs_kernel(mix_ref, x_ref, r_ref, p_ref, resid_ref, x_out, p_out):
    k = x_ref.shape[0]
    resid = jnp.concatenate([resid_ref[i] for i in range(resid_ref.shape[0])], 1)
    vectors = jnp.concatenate([x_ref[...], r_ref[...], p_ref[...], resid], 0)
    out = three(split(mix_ref[...]), split(vectors), TN)
    x_out[...] = out[:k]
    p_out[...] = out[k:]


def residual_kernel(turn_ref, prods_ref, a_ref, b_ref, out_ref, first_ref, second_ref):
    pieces, _, lanes = prods_ref.shape
    k = turn_ref.shape[1]

    @pl.when(pl.program_id(0) == 0)
    def _():
        turn = split(turn_ref[...])
        for i in range(pieces):
            block = three(split(prods_ref[i]), turn, TN)
            high = block.astype(jnp.bfloat16).astype(jnp.float32)
            low = block - high
            rows = pl.ds(i * lanes, lanes)
            first_ref[rows, :] = jnp.concatenate([high, low], 1).astype(jnp.bfloat16)
            second_ref[rows, :] = jnp.concatenate([low, high], 1).astype(jnp.bfloat16)

    sums = []
    for ref, parts_ref in ((a_ref, first_ref), (b_ref, second_ref)):
        high, low = split(ref[...])
        part = jnp.dot(high, parts_ref[...], preferred_element_type=jnp.float32) + jnp.dot(
            low, parts_ref[...], preferred_element_type=jnp.float32
        )
        sums.append(part + pltpu.roll(part, k, 1))
    lane = lax.broadcasted_iota(jnp.int32, sums[0].shape, 1)
    out_ref[...] = jnp.where(lane < k, sums[0], sums[1])


def products(x, r, p, a, b, pieces):
    k, rows = x.shape
    lanes = a.shape[1] // pieces
    each = 2
    block = pl.BlockSpec((k, rows), lambda i: (0, 0))
    tile = pl.BlockSpec((rows, each * lanes), lambda i: (0, i))
    return pl.pallas_call(
        products_kernel,
        grid=(pieces // each,),
        in_specs=[block, block, block, tile, tile],
        out_specs=pl.BlockSpec((each, 6 * k, lanes), lambda i: (i, 0, 0)),
        out_shape=f32(pieces, 6 * k, lanes),
        scratch_shapes=[pltpu.VMEM((6 * k, rows), jnp.bfloat16)],
        compiler_params=pltpu.CompilerParams(vmem_limit_bytes=60 * 2**20),
        cost_estimate=cost(1e10, 8 * rows * a.shape[1]),
        name="products",
    )(x, r, p, a, b)


def residual_products(turn, prods, a, b):
    k = turn.shape[1]
    rows, cols = a.shape
    height = 512
    tile = pl.BlockSpec((height, cols), lambda i: (i, 0))
    return pl.pallas_call(
        residual_kernel,
        grid=(rows // height,),
        in_specs=[
            pl.BlockSpec(turn.shape, lambda i: (0, 0)),
            pl.BlockSpec(prods.shape, lambda i: (0, 0, 0)),
            tile,
            tile,
        ],
        out_specs=pl.BlockSpec((height, 2 * k), lambda i: (i, 0)),
        out_shape=f32(rows, 2 * k),
        scratch_shapes=[pltpu.VMEM((cols, 2 * k), jnp.bfloat16)] * 2,
        compiler_params=pltpu.CompilerParams(vmem_limit_bytes=60 * 2**20),
        cost_estimate=cost(1e10, 8 * rows * cols),
        name="residual_products",
    )(turn, prods, a, b)


def outputs(mix, x, r, p, resid):
    k, rows = x.shape
    pieces, _, lanes = resid.shape
    each = 8
    part = pl.BlockSpec((k, each * lanes), lambda i: (0, i))
    return pl.pallas_call(
        outputs_kernel,
        grid=(pieces // each,),
        in_specs=[
            pl.BlockSpec(mix.shape, lambda i: (0, 0)),
            part,
            part,
            part,
            pl.BlockSpec((each, k, lanes), lambda i: (i, 0, 0)),
        ],
        out_specs=(part, part),
        out_shape=(f32(k, rows), f32(k, rows)),
        compiler_params=pltpu.CompilerParams(vmem_limit_bytes=60 * 2**20),
        cost_estimate=cost(3e9, 40 * rows * k),
        name="outputs",
    )(mix, x, r, p, resid)


def local(a_matrix, b_matrix, x_block, r_block, p_block):
    rows, cols = lax.axis_size("row"), lax.axis_size("col")
    count = rows * cols
    k = x_block.shape[1]
    order = x_block.shape[0] * rows
    piece = order // count
    to_col = [(b, (b % rows) * cols + b // rows) for b in range(count)]
    to_row = [(d, s) for s, d in to_col]

    panel = [x_block.T, r_block.T, p_block.T]
    start = lax.axis_index("col") * piece
    own_row = jnp.concatenate(
        [lax.dynamic_slice_in_dim(x, start, piece, 1) for x in panel], 0
    )
    own_col = lax.ppermute(own_row, BOTH, to_col)

    prods = products(*panel, a_matrix, b_matrix, rows)
    prods = lax.all_to_all(prods, "row", 0, 0)
    prod_col, packed = call(
        gram_kernel, "gram", (f32(6 * k, piece), f32(6 * k, 2 * k)), [], 2e9, prods, own_col
    )
    prod_row = lax.ppermute(prod_col, BOTH, to_row)
    prods_col = lax.all_gather(prod_col, "row")
    packed = sum_everywhere(packed)
    turn, basis, old = call(
        functools.partial(first_kernel, k, order),
        "ritz_first",
        (f32(6 * k, k), f32(3 * k, 2 * k), f32(4 * k, 2 * k)),
        [(3 * k, 3 * k)] * 3,
        1.7e10,
        packed,
    )
    turn, prod_row = lax.optimization_barrier((turn, prod_row))

    parts = residual_products(turn, prods_col, a_matrix, b_matrix)
    parts = lax.all_to_all(parts.reshape(cols, piece, 2 * k), "col", 0, 0)
    more_row, resid_row, fresh = call(
        fresh_kernel,
        "fresh",
        (f32(piece, 2 * k), f32(2 * k, piece), f32(3 * k, 2 * k)),
        [],
        1e9,
        parts,
        turn,
        prod_row,
        basis,
        own_row,
    )
    resid = lax.all_gather(resid_row, "col")
    fresh = sum_everywhere(fresh)
    r_own, mix = call(
        functools.partial(second_kernel, k, order),
        "ritz_second",
        (f32(k, piece), f32(4 * k, 2 * k)),
        [(3 * k, 3 * k)] * 2,
        1.7e10,
        old,
        fresh,
        basis,
        prod_row,
        more_row,
    )
    r_next = share(r_own, "col")
    x_next, p_next = outputs(mix, *panel, resid)
    r_next, x_next, p_next = lax.optimization_barrier((r_next, x_next, p_next))
    r_next = r_next.transpose(1, 0, 2).reshape(k, -1)
    return (x_next.T, r_next.T, p_next.T)


def solution(mesh):
    return jax.shard_map(
        local,
        mesh=mesh,
        in_specs=(P("row", "col"), P("row", "col"), P("row", None), P("row", None), P("row", None)),
        out_specs=(P("row", None), P("row", None), P("row", None)),
        check_vma=False,
    )
```

```python
import functools
import math

import jax
import jax.numpy as jnp
from jax import lax
from jax.experimental import pallas as pl
from jax.experimental.pallas import tpu as pltpu
from jax.sharding import PartitionSpec as P

NS_STEPS = 8
BOTH = ("row", "col")


def mm(left, right, dims=((1,), (0,)), precision=lax.Precision.HIGHEST):
    return lax.dot_general(
        left, right, (dims, ((), ())), precision=precision, preferred_element_type=jnp.float32
    )


def share(x, axis):
    copies = jnp.broadcast_to(x[None], (lax.axis_size(axis),) + x.shape)
    return lax.all_to_all(copies, axis, 0, 0)


def sum_everywhere(x):
    parts = x.reshape(lax.axis_size("row"), -1, x.shape[-1])
    own = lax.all_to_all(parts, "row", 0, 0).sum(0)
    own = share(own, "col").sum(0)
    return share(own, "row").reshape(x.shape)


def dot(left, right, dims=((1,), (0,))):
    return lax.dot_general(
        left, right, (dims, ((), ())),
        precision=lax.Precision.HIGHEST, preferred_element_type=jnp.float32,
    )


NT = ((1,), (1,))
TN = ((0,), (0,))


def split(x):
    high = x.astype(jnp.bfloat16)
    return high, (x - high.astype(jnp.float32)).astype(jnp.bfloat16)


def dot3(left, right):
    def one(a, b):
        return jnp.dot(a, b, preferred_element_type=jnp.float32)

    return one(left[0], right[1]) + one(left[1], right[0]) + one(left[0], right[0])


def inverse_factor(block):
    k = block.shape[0]
    height = 8
    diag = lax.broadcasted_iota(jnp.int32, (k, k), 0) == lax.broadcasted_iota(jnp.int32, (k, k), 1)
    wide = jnp.concatenate([block, diag.astype(jnp.float32)], 1)
    full = (height, 2 * k)
    strips = [wide[i : i + height] for i in range(0, k, height)]
    line = lax.broadcasted_iota(jnp.int32, full, 0)
    done = []
    for at in range(k // height):
        first = at * height
        rows = [jnp.broadcast_to(strips[at][i : i + 1], full) for i in range(height)]
        elem = [
            [jnp.broadcast_to(rows[m][:, first + i : first + i + 1], full) for i in range(m + 1)]
            for m in range(height)
        ]
        later = range(at + 1, k // height)
        cols = {
            t: [
                jnp.broadcast_to(strips[t][:, first + i : first + i + 1], full)
                for i in range(height)
            ]
            for t in later
        }
        low = [[None] * height for _ in range(height)]
        inv = {}
        out = None
        for i in range(0, height, 2):
            a, b, c = elem[i][i], elem[i + 1][i], elem[i + 1][i + 1]
            det = a * c - b * b
            inv[i] = 1.0 / det
            for m in range(i + 2, height):
                u, v = elem[m][i], elem[m][i + 1]
                low[m][i] = (u * c - v * b) * inv[i]
                low[m][i + 1] = (v * a - u * b) * inv[i]
                for n in range(i + 2, m + 1):
                    elem[m][n] = elem[m][n] - (
                        low[m][i] * elem[n][i] + low[m][i + 1] * elem[n][i + 1]
                    )
                rows[m] = rows[m] - (low[m][i] * rows[i] + low[m][i + 1] * rows[i + 1])
            scale = 1.0 / a
            upper = rows[i] * (1.0 / jnp.sqrt(a))
            lower = (rows[i + 1] - (b * scale) * rows[i]) * (1.0 / jnp.sqrt(det * scale))
            out = upper if out is None else jnp.where(line == i, upper, out)
            out = jnp.where(line == i + 1, lower, out)
        done.append(out)
        if not later:
            break
        solved = [None] * height
        for i in reversed(range(0, height, 2)):
            a, b, c = elem[i][i], elem[i + 1][i], elem[i + 1][i + 1]
            solved[i] = (c * rows[i] - b * rows[i + 1]) * inv[i]
            solved[i + 1] = (a * rows[i + 1] - b * rows[i]) * inv[i]
            for m in range(i + 2, height):
                solved[i] = solved[i] - low[m][i] * solved[m]
                solved[i + 1] = solved[i + 1] - low[m][i + 1] * solved[m]
        for t in later:
            for m in range(height):
                strips[t] = strips[t] - cols[t][m] * solved[m]
    return jnp.concatenate(done, 0)[:, k:]


def ritz_step(k, order, blocks_b, whole_a, inv_ref):
    b00, b10, b11, b20, b21, b22 = blocks_b
    t0 = inverse_factor(b00)
    l10 = dot(b10, t0, NT)
    l20 = dot(b20, t0, NT)
    t1 = inverse_factor(b11 - dot(l10, l10, NT))
    l21 = dot(b21 - dot(l20, l10, NT), t1, NT)
    t2 = inverse_factor(b22 - dot(l20, l20, NT) - dot(l21, l21, NT))
    t10 = -dot(t1, dot(l10, t0))
    t20 = -dot(t2, dot(l20, t0) + dot(l21, t10))
    t21 = -dot(t2, dot(l21, t1))
    inv_ref[...] = jnp.zeros_like(inv_ref)
    inv_ref[:k, :k] = t0
    inv_ref[k : 2 * k, :k] = t10
    inv_ref[k : 2 * k, k : 2 * k] = t1
    inv_ref[2 * k :, : 2 * k] = jnp.concatenate([t20, t21], 1)
    inv_ref[2 * k :, 2 * k :] = t2
    inverse = inv_ref[...]
    middle = dot(dot(inverse, whole_a), inverse, NT)
    middle = 0.5 * (middle + middle.T)
    size = 3 * k
    diag = lax.broadcasted_iota(jnp.int32, (size, size), 0) == lax.broadcasted_iota(
        jnp.int32, (size, size), 1
    )

    def total(x):
        return jnp.sum(jnp.sum(x, 0, keepdims=True), 1, keepdims=True)

    shift = total(jnp.where(diag, middle, 0.0)) * (1.0 / size)
    sign = middle - jnp.where(diag, shift, 0.0)
    sign = sign * (1.0 / jnp.sqrt(total(sign * sign) + 1e-06))
    for turn in range(NS_STEPS):
        parts = split(sign)
        sign = 1.5 * sign - 0.5 * dot3(parts, split(dot3(parts, parts)))
    filtered = 0.5 * (jnp.where(diag, 1.0, 0.0) - sign)[:, :k]
    coords = dot(inverse, filtered, TN) * math.sqrt(order)
    reduced = dot(filtered, dot(middle, filtered), TN)
    return coords, reduced


def put_whole(ref, blocks, k):
    b00, b10, b11, b20, b21, b22 = blocks
    ref[:k, : 2 * k] = jnp.concatenate([b00, b10.T], 1)
    ref[:k, 2 * k :] = b20.T
    ref[k : 2 * k, : 2 * k] = jnp.concatenate([b10, b11], 1)
    ref[k : 2 * k, 2 * k :] = b21.T
    ref[2 * k :, : 2 * k] = jnp.concatenate([b20, b21], 1)
    ref[2 * k :, 2 * k :] = b22
    return ref[...]


def first_kernel(k, order, packed_ref, turn_ref, basis_ref, inv_ref, a_ref):
    blocks = [packed_ref[i * k : (i + 1) * k] for i in range(6)]
    whole_a = put_whole(a_ref, [x[:, :k] for x in blocks], k)
    coords, reduced = ritz_step(k, order, [x[:, k:] for x in blocks], whole_a, inv_ref)
    turn_ref[: 3 * k] = coords
    turn_ref[3 * k :] = -dot(coords, reduced)
    basis_ref[:k] = jnp.concatenate([coords[:k], jnp.zeros((k, k), jnp.float32)], 1)
    basis_ref[k:] = jnp.concatenate([coords[k:], coords[k:]], 1)


def kept_kernel(packed_ref, basis_ref, old_ref, whole_ref):
    k = basis_ref.shape[1] // 2
    blocks = [packed_ref[i * k : (i + 1) * k] for i in range(6)]
    basis = basis_ref[...]
    for i in range(2):
        whole = put_whole(whole_ref, [x[:, i * k : (i + 1) * k] for x in blocks], k)
        old_ref[i * 2 * k : (i + 1) * 2 * k] = dot(basis, dot(whole, basis), TN)


def second_kernel(
    k,
    order,
    old_ref,
    fresh_ref,
    basis_ref,
    prod_ref,
    more_ref,
    r_ref,
    mix_ref,
    inv_ref,
    a_ref,
):
    def blocks(old, new):
        mid = new[k : 2 * k]
        return [
            old[:k, :k],
            new[:k].T,
            0.5 * (mid + mid.T),
            old[k:, :k],
            new[2 * k :],
            old[k:, k:],
        ]

    whole_a = put_whole(a_ref, blocks(old_ref[: 2 * k], fresh_ref[:, :k]), k)
    blocks_b = blocks(old_ref[2 * k :], fresh_ref[:, k:])
    coords, reduced = ritz_step(k, order, blocks_b, whole_a, inv_ref)
    basis = basis_ref[...]
    from_r = coords[k : 2 * k]
    move_p = dot(basis[:, k:], coords[2 * k :])
    move_x = dot(basis, jnp.concatenate([coords[:k], coords[2 * k :]], 0))
    more = more_ref[...].T
    mix_ref[: 3 * k] = jnp.concatenate([move_x, move_p], 1)
    mix_ref[3 * k :] = jnp.concatenate([from_r, from_r], 1)
    resid = (
        dot(move_x, prod_ref[: 3 * k], TN)
        - dot(dot(move_x, reduced), prod_ref[3 * k :], TN)
        + dot(from_r, more[:k], TN)
        - dot(dot(from_r, reduced), more[k:], TN)
    )
    for i in range(r_ref.shape[0]):
        r_ref[i] = resid


def f32(*shape):
    return jax.ShapeDtypeStruct(shape, jnp.float32)


def cost(flops, size):
    return pl.CostEstimate(flops=int(flops), bytes_accessed=int(size), transcendentals=0)


def call(kernel, name, out_shape, scratch, flops, *args):
    return pl.pallas_call(
        kernel,
        out_shape=out_shape,
        scratch_shapes=[pltpu.VMEM(shape, jnp.float32) for shape in scratch],
        compiler_params=pltpu.CompilerParams(vmem_limit_bytes=32 * 2**20),
        cost_estimate=cost(flops, 2**20),
        name=name,
    )(*args)


def three(left, right, dims):
    def one(a, b):
        return lax.dot_general(a, b, (dims, ((), ())), preferred_element_type=jnp.float32)

    return one(left[0], right[1]) + one(left[1], right[0]) + one(left[0], right[0])


def products_kernel(x_ref, r_ref, p_ref, a_ref, b_ref, out_ref, panel_ref):
    k = x_ref.shape[0]
    wide = 3 * k

    @pl.when(pl.program_id(0) == 0)
    def _():
        for i, ref in enumerate((x_ref, r_ref, p_ref)):
            high, low = split(ref[...])
            panel_ref[i * k : (i + 1) * k] = high
            panel_ref[wide + i * k : wide + (i + 1) * k] = low

    def one(a, b):
        return jnp.dot(a, b, preferred_element_type=jnp.float32)

    for at, ref in ((0, a_ref), (wide, b_ref)):
        high, low = split(ref[...])
        both = one(panel_ref[...], high)
        prod = both[:wide] + both[wide:] + one(panel_ref[:wide], low)
        for i in range(out_ref.shape[0]):
            lanes = out_ref.shape[2]
            out_ref[i, at : at + wide] = prod[:, i * lanes : (i + 1) * lanes]


def gram_kernel(parts_ref, panel_ref, prods_ref, out_ref):
    wide = panel_ref.shape[0]
    k = wide // 3
    prods = parts_ref[0]
    for i in range(1, parts_ref.shape[0]):
        prods = prods + parts_ref[i]
    prods_ref[...] = prods
    gram = three(split(prods), split(panel_ref[...]), NT)
    at = 0
    for i in range(3):
        for j in range(i + 1):
            pair = []
            for base in (0, wide):
                block = gram[base + i * k : base + (i + 1) * k, j * k : (j + 1) * k]
                other = gram[base + j * k : base + (j + 1) * k, i * k : (i + 1) * k]
                pair.append(0.5 * (block + other.T))
            out_ref[at : at + k] = jnp.concatenate(pair, 1)
            at += k


def tests_kernel(turn_ref, prods_ref, basis_ref, own_ref, out_ref, resid_ref):
    k = turn_ref.shape[1]
    resid = dot(turn_ref[...], prods_ref[...], TN)
    resid_ref[:k] = resid
    resid_ref[k:] = jnp.zeros_like(resid)
    kept = dot(basis_ref[...], own_ref[...], TN)
    out_ref[:k] = kept[:k]
    out_ref[k : 2 * k] = resid
    out_ref[2 * k :] = kept[k:]


def fresh_kernel(parts_ref, tests_ref, more_ref, out_ref):
    more = parts_ref[0]
    for i in range(1, parts_ref.shape[0]):
        more = more + parts_ref[i]
    more_ref[...] = more
    out_ref[...] = three(split(tests_ref[...]), split(more), ((1,), (0,)))


def outputs_kernel(mix_ref, x_ref, r_ref, p_ref, resid_ref, x_out, p_out):
    k = x_ref.shape[0]
    resid = jnp.concatenate([resid_ref[i] for i in range(resid_ref.shape[0])], 1)
    vectors = jnp.concatenate([x_ref[...], r_ref[...], p_ref[...], resid], 0)
    out = three(split(mix_ref[...]), split(vectors), TN)
    x_out[...] = out[:k]
    p_out[...] = out[k:]


def residual_kernel(turn_ref, prods_ref, a_ref, b_ref, out_ref, first_ref, second_ref):
    pieces, _, lanes = prods_ref.shape
    k = turn_ref.shape[1]

    @pl.when(pl.program_id(0) == 0)
    def _():
        turn = split(turn_ref[...])
        for i in range(pieces):
            block = three(split(prods_ref[i]), turn, TN)
            high = block.astype(jnp.bfloat16).astype(jnp.float32)
            low = block - high
            rows = pl.ds(i * lanes, lanes)
            first_ref[rows, :] = jnp.concatenate([high, low], 1).astype(jnp.bfloat16)
            second_ref[rows, :] = jnp.concatenate([low, high], 1).astype(jnp.bfloat16)

    sums = []
    for ref, parts_ref in ((a_ref, first_ref), (b_ref, second_ref)):
        high, low = split(ref[...])
        part = jnp.dot(high, parts_ref[...], preferred_element_type=jnp.float32) + jnp.dot(
            low, parts_ref[...], preferred_element_type=jnp.float32
        )
        sums.append(part + pltpu.roll(part, k, 1))
    lane = lax.broadcasted_iota(jnp.int32, sums[0].shape, 1)
    out_ref[...] = jnp.where(lane < k, sums[0], sums[1])


def products(x, r, p, a, b, pieces):
    k, rows = x.shape
    lanes = a.shape[1] // pieces
    each = 2
    block = pl.BlockSpec((k, rows), lambda i: (0, 0))
    tile = pl.BlockSpec((rows, each * lanes), lambda i: (0, i))
    return pl.pallas_call(
        products_kernel,
        grid=(pieces // each,),
        in_specs=[block, block, block, tile, tile],
        out_specs=pl.BlockSpec((each, 6 * k, lanes), lambda i: (i, 0, 0)),
        out_shape=f32(pieces, 6 * k, lanes),
        scratch_shapes=[pltpu.VMEM((6 * k, rows), jnp.bfloat16)],
        compiler_params=pltpu.CompilerParams(vmem_limit_bytes=60 * 2**20),
        cost_estimate=cost(1e10, 8 * rows * a.shape[1]),
        name="products",
    )(x, r, p, a, b)


def residual_products(turn, prods, a, b):
    k = turn.shape[1]
    rows, cols = a.shape
    height = 512
    tile = pl.BlockSpec((height, cols), lambda i: (i, 0))
    return pl.pallas_call(
        residual_kernel,
        grid=(rows // height,),
        in_specs=[
            pl.BlockSpec(turn.shape, lambda i: (0, 0)),
            pl.BlockSpec(prods.shape, lambda i: (0, 0, 0)),
            tile,
            tile,
        ],
        out_specs=pl.BlockSpec((height, 2 * k), lambda i: (i, 0)),
        out_shape=f32(rows, 2 * k),
        scratch_shapes=[pltpu.VMEM((cols, 2 * k), jnp.bfloat16)] * 2,
        compiler_params=pltpu.CompilerParams(vmem_limit_bytes=60 * 2**20),
        cost_estimate=cost(1e10, 8 * rows * cols),
        name="residual_products",
    )(turn, prods, a, b)


def outputs(mix, x, r, p, resid):
    k, rows = x.shape
    pieces, _, lanes = resid.shape
    each = 8
    part = pl.BlockSpec((k, each * lanes), lambda i: (0, i))
    return pl.pallas_call(
        outputs_kernel,
        grid=(pieces // each,),
        in_specs=[
            pl.BlockSpec(mix.shape, lambda i: (0, 0)),
            part,
            part,
            part,
            pl.BlockSpec((each, k, lanes), lambda i: (i, 0, 0)),
        ],
        out_specs=(part, part),
        out_shape=(f32(k, rows), f32(k, rows)),
        compiler_params=pltpu.CompilerParams(vmem_limit_bytes=60 * 2**20),
        cost_estimate=cost(3e9, 40 * rows * k),
        name="outputs",
    )(mix, x, r, p, resid)


def local(a_matrix, b_matrix, x_block, r_block, p_block):
    rows, cols = lax.axis_size("row"), lax.axis_size("col")
    count = rows * cols
    k = x_block.shape[1]
    order = x_block.shape[0] * rows
    piece = order // count
    to_col = [(b, (b % rows) * cols + b // rows) for b in range(count)]
    to_row = [(d, s) for s, d in to_col]

    panel = [x_block.T, r_block.T, p_block.T]
    start = lax.axis_index("col") * piece
    own_row = jnp.concatenate(
        [lax.dynamic_slice_in_dim(x, start, piece, 1) for x in panel], 0
    )
    own_col = lax.ppermute(own_row, BOTH, to_col)

    prods = products(*panel, a_matrix, b_matrix, rows)
    prods = lax.all_to_all(prods, "row", 0, 0)
    prod_col, packed = call(
        gram_kernel, "gram", (f32(6 * k, piece), f32(6 * k, 2 * k)), [], 2e9, prods, own_col
    )
    prod_row = lax.ppermute(prod_col, BOTH, to_row)
    prods_col = lax.all_gather(prod_col, "row")
    packed = sum_everywhere(packed)
    turn, basis = call(
        functools.partial(first_kernel, k, order),
        "ritz_first",
        (f32(6 * k, k), f32(3 * k, 2 * k)),
        [(3 * k, 3 * k)] * 2,
        1.7e10,
        packed,
    )
    turn, prod_row = lax.optimization_barrier((turn, prod_row))

    parts = residual_products(turn, prods_col, a_matrix, b_matrix)
    parts = lax.all_to_all(parts.reshape(cols, piece, 2 * k), "col", 0, 0)
    old = call(kept_kernel, "kept", f32(4 * k, 2 * k), [(3 * k, 3 * k)], 3e9, packed, basis)
    tests, resid_row = call(
        tests_kernel,
        "tests",
        (f32(3 * k, piece), f32(2 * k, piece)),
        [],
        1e9,
        turn,
        prod_row,
        basis,
        own_row,
    )
    more_row, fresh = call(
        fresh_kernel, "fresh", (f32(piece, 2 * k), f32(3 * k, 2 * k)), [], 1e9, parts, tests
    )
    fresh, resid_row = lax.optimization_barrier((fresh, resid_row))
    resid = lax.all_gather(resid_row, "col")
    fresh = sum_everywhere(fresh)
    r_own, mix = call(
        functools.partial(second_kernel, k, order),
        "ritz_second",
        (f32(cols, k, piece), f32(4 * k, 2 * k)),
        [(3 * k, 3 * k)] * 2,
        1e7,
        old,
        fresh,
        basis,
        prod_row,
        more_row,
    )
    r_next = lax.all_to_all(r_own, "col", 0, 0)
    x_next, p_next = outputs(mix, *panel, resid)
    r_next, x_next, p_next = lax.optimization_barrier((r_next, x_next, p_next))
    r_next = r_next.transpose(1, 0, 2).reshape(k, -1)
    return (x_next.T, r_next.T, p_next.T)


def solution(mesh):
    return jax.shard_map(
        local,
        mesh=mesh,
        in_specs=(P("row", "col"), P("row", "col"), P("row", None), P("row", None), P("row", None)),
        out_specs=(P("row", None), P("row", None), P("row", None)),
        check_vma=False,
    )
```

```python
import functools
import math

import jax
import jax.numpy as jnp
from jax import lax
from jax.experimental import pallas as pl
from jax.experimental.pallas import tpu as pltpu
from jax.sharding import PartitionSpec as P

NS_STEPS = 8
BOTH = ("row", "col")


def mm(left, right, dims=((1,), (0,)), precision=lax.Precision.HIGHEST):
    return lax.dot_general(
        left, right, (dims, ((), ())), precision=precision, preferred_element_type=jnp.float32
    )


def share(x, axis):
    copies = jnp.broadcast_to(x[None], (lax.axis_size(axis),) + x.shape)
    return lax.all_to_all(copies, axis, 0, 0)


def sum_everywhere(x):
    parts = x.reshape(lax.axis_size("row"), -1, x.shape[-1])
    own = lax.all_to_all(parts, "row", 0, 0).sum(0)
    own = share(own, "col").sum(0)
    return share(own, "row").reshape(x.shape)


def dot(left, right, dims=((1,), (0,))):
    return lax.dot_general(
        left, right, (dims, ((), ())),
        precision=lax.Precision.HIGHEST, preferred_element_type=jnp.float32,
    )


NT = ((1,), (1,))
TN = ((0,), (0,))


def split(x):
    high = x.astype(jnp.bfloat16)
    return high, (x - high.astype(jnp.float32)).astype(jnp.bfloat16)


def dot3(left, right):
    def one(a, b):
        return jnp.dot(a, b, preferred_element_type=jnp.float32)

    return one(left[0], right[1]) + one(left[1], right[0]) + one(left[0], right[0])


def inverse_factor(block):
    k = block.shape[0]
    height = 8
    diag = lax.broadcasted_iota(jnp.int32, (k, k), 0) == lax.broadcasted_iota(jnp.int32, (k, k), 1)
    wide = jnp.concatenate([block, diag.astype(jnp.float32)], 1)
    full = (height, 2 * k)
    strips = [wide[i : i + height] for i in range(0, k, height)]
    line = lax.broadcasted_iota(jnp.int32, full, 0)
    done = []
    for at in range(k // height):
        first = at * height
        rows = [jnp.broadcast_to(strips[at][i : i + 1], full) for i in range(height)]
        elem = [
            [jnp.broadcast_to(rows[m][:, first + i : first + i + 1], full) for i in range(m + 1)]
            for m in range(height)
        ]
        later = range(at + 1, k // height)
        cols = {
            t: [
                jnp.broadcast_to(strips[t][:, first + i : first + i + 1], full)
                for i in range(height)
            ]
            for t in later
        }
        low = [[None] * height for _ in range(height)]
        inv = {}
        out = None
        for i in range(0, height, 2):
            a, b, c = elem[i][i], elem[i + 1][i], elem[i + 1][i + 1]
            det = a * c - b * b
            inv[i] = 1.0 / det
            for m in range(i + 2, height):
                u, v = elem[m][i], elem[m][i + 1]
                low[m][i] = (u * c - v * b) * inv[i]
                low[m][i + 1] = (v * a - u * b) * inv[i]
                for n in range(i + 2, m + 1):
                    elem[m][n] = elem[m][n] - (
                        low[m][i] * elem[n][i] + low[m][i + 1] * elem[n][i + 1]
                    )
                rows[m] = rows[m] - (low[m][i] * rows[i] + low[m][i + 1] * rows[i + 1])
            scale = 1.0 / a
            upper = rows[i] * (1.0 / jnp.sqrt(a))
            lower = (rows[i + 1] - (b * scale) * rows[i]) * (1.0 / jnp.sqrt(det * scale))
            out = upper if out is None else jnp.where(line == i, upper, out)
            out = jnp.where(line == i + 1, lower, out)
        done.append(out)
        if not later:
            break
        solved = [None] * height
        for i in reversed(range(0, height, 2)):
            a, b, c = elem[i][i], elem[i + 1][i], elem[i + 1][i + 1]
            solved[i] = (c * rows[i] - b * rows[i + 1]) * inv[i]
            solved[i + 1] = (a * rows[i + 1] - b * rows[i]) * inv[i]
            for m in range(i + 2, height):
                solved[i] = solved[i] - low[m][i] * solved[m]
                solved[i + 1] = solved[i + 1] - low[m][i + 1] * solved[m]
        for t in later:
            for m in range(height):
                strips[t] = strips[t] - cols[t][m] * solved[m]
    return jnp.concatenate(done, 0)[:, k:]


def ritz_step(k, order, blocks_b, whole_a, inv_ref):
    b00, b10, b11, b20, b21, b22 = blocks_b
    t0 = inverse_factor(b00)
    l10 = dot(b10, t0, NT)
    l20 = dot(b20, t0, NT)
    t1 = inverse_factor(b11 - dot(l10, l10, NT))
    l21 = dot(b21 - dot(l20, l10, NT), t1, NT)
    t2 = inverse_factor(b22 - dot(l20, l20, NT) - dot(l21, l21, NT))
    t10 = -dot(t1, dot(l10, t0))
    t20 = -dot(t2, dot(l20, t0) + dot(l21, t10))
    t21 = -dot(t2, dot(l21, t1))
    inv_ref[...] = jnp.zeros_like(inv_ref)
    inv_ref[:k, :k] = t0
    inv_ref[k : 2 * k, :k] = t10
    inv_ref[k : 2 * k, k : 2 * k] = t1
    inv_ref[2 * k :, : 2 * k] = jnp.concatenate([t20, t21], 1)
    inv_ref[2 * k :, 2 * k :] = t2
    inverse = inv_ref[...]
    middle = dot(dot(inverse, whole_a), inverse, NT)
    middle = 0.5 * (middle + middle.T)
    size = 3 * k
    diag = lax.broadcasted_iota(jnp.int32, (size, size), 0) == lax.broadcasted_iota(
        jnp.int32, (size, size), 1
    )

    def total(x):
        return jnp.sum(jnp.sum(x, 0, keepdims=True), 1, keepdims=True)

    shift = total(jnp.where(diag, middle, 0.0)) * (1.0 / size)
    sign = middle - jnp.where(diag, shift, 0.0)
    sign = sign * (1.0 / jnp.sqrt(total(sign * sign) + 1e-06))
    for turn in range(NS_STEPS):
        parts = split(sign)
        sign = 1.5 * sign - 0.5 * dot3(parts, split(dot3(parts, parts)))
    filtered = 0.5 * (jnp.where(diag, 1.0, 0.0) - sign)[:, :k]
    coords = dot(inverse, filtered, TN) * math.sqrt(order)
    reduced = dot(filtered, dot(middle, filtered), TN)
    return coords, reduced


def put_whole(ref, blocks, k):
    b00, b10, b11, b20, b21, b22 = blocks
    ref[:k, : 2 * k] = jnp.concatenate([b00, b10.T], 1)
    ref[:k, 2 * k :] = b20.T
    ref[k : 2 * k, : 2 * k] = jnp.concatenate([b10, b11], 1)
    ref[k : 2 * k, 2 * k :] = b21.T
    ref[2 * k :, : 2 * k] = jnp.concatenate([b20, b21], 1)
    ref[2 * k :, 2 * k :] = b22
    return ref[...]


def first_kernel(
    k,
    order,
    packed_ref,
    prods_ref,
    a_hbm,
    b_hbm,
    turn_ref,
    basis_ref,
    out_ref,
    inv_ref,
    whole_ref,
    a_ref,
    b_ref,
    high_ref,
    low_ref,
    sems,
):
    copies = [
        pltpu.make_async_copy(a_hbm, a_ref, sems.at[0]),
        pltpu.make_async_copy(b_hbm, b_ref, sems.at[1]),
    ]
    for copy in copies:
        copy.start()
    blocks = [packed_ref[i * k : (i + 1) * k] for i in range(6)]
    whole_a = put_whole(whole_ref, [x[:, :k] for x in blocks], k)
    coords, reduced = ritz_step(k, order, [x[:, k:] for x in blocks], whole_a, inv_ref)
    turn_ref[: 3 * k] = coords
    turn_ref[3 * k :] = -dot(coords, reduced)
    basis_ref[:k] = jnp.concatenate([coords[:k], jnp.zeros((k, k), jnp.float32)], 1)
    basis_ref[k:] = jnp.concatenate([coords[k:], coords[k:]], 1)

    pieces, _, lanes = prods_ref.shape
    turn = split(turn_ref[...])
    for i in range(pieces):
        block = three(turn, split(prods_ref[i]), TN).T
        high = block.astype(jnp.bfloat16).astype(jnp.float32)
        low = block - high
        high_ref[i * lanes : (i + 1) * lanes] = jnp.concatenate([high, low], 1).astype(jnp.bfloat16)
        low_ref[i * lanes : (i + 1) * lanes] = jnp.concatenate([low, high], 1).astype(jnp.bfloat16)
    for copy in copies:
        copy.wait()
    height = 256
    lane = lax.broadcasted_iota(jnp.int32, (height, 2 * k), 1)

    @pl.loop(0, out_ref.shape[0] // height, unroll=8)
    def _(step):
        rows = pl.ds(pl.multiple_of(step * height, height), height)
        sums = []
        for ref, parts_ref in ((a_ref, high_ref), (b_ref, low_ref)):
            high, low = split(ref[rows, :])
            part = jnp.dot(high, parts_ref[...], preferred_element_type=jnp.float32) + jnp.dot(
                low, parts_ref[...], preferred_element_type=jnp.float32
            )
            sums.append(part + pltpu.roll(part, k, 1))
        out_ref[rows, :] = jnp.where(lane < k, sums[0], sums[1])


def kept_kernel(packed_ref, basis_ref, old_ref, whole_ref):
    k = basis_ref.shape[1] // 2
    blocks = [packed_ref[i * k : (i + 1) * k] for i in range(6)]
    basis = basis_ref[...]
    for i in range(2):
        whole = put_whole(whole_ref, [x[:, i * k : (i + 1) * k] for x in blocks], k)
        old_ref[i * 2 * k : (i + 1) * 2 * k] = dot(basis, dot(whole, basis), TN)


def second_kernel(
    k,
    order,
    old_ref,
    fresh_ref,
    basis_ref,
    prod_ref,
    more_ref,
    r_ref,
    mix_ref,
    inv_ref,
    a_ref,
):
    def blocks(old, new):
        mid = new[k : 2 * k]
        return [
            old[:k, :k],
            new[:k].T,
            0.5 * (mid + mid.T),
            old[k:, :k],
            new[2 * k :],
            old[k:, k:],
        ]

    whole_a = put_whole(a_ref, blocks(old_ref[: 2 * k], fresh_ref[:, :k]), k)
    blocks_b = blocks(old_ref[2 * k :], fresh_ref[:, k:])
    coords, reduced = ritz_step(k, order, blocks_b, whole_a, inv_ref)
    basis = basis_ref[...]
    from_r = coords[k : 2 * k]
    move_p = dot(basis[:, k:], coords[2 * k :])
    move_x = dot(basis, jnp.concatenate([coords[:k], coords[2 * k :]], 0))
    more = more_ref[...].T
    mix_ref[: 3 * k] = jnp.concatenate([move_x, move_p], 1)
    mix_ref[3 * k :] = jnp.concatenate([from_r, from_r], 1)
    resid = (
        dot(move_x, prod_ref[: 3 * k], TN)
        - dot(dot(move_x, reduced), prod_ref[3 * k :], TN)
        + dot(from_r, more[:k], TN)
        - dot(dot(from_r, reduced), more[k:], TN)
    )
    for i in range(r_ref.shape[0]):
        r_ref[i] = resid


def f32(*shape):
    return jax.ShapeDtypeStruct(shape, jnp.float32)


def cost(flops, size):
    return pl.CostEstimate(flops=int(flops), bytes_accessed=int(size), transcendentals=0)


def call(kernel, name, out_shape, scratch, flops, *args):
    return pl.pallas_call(
        kernel,
        out_shape=out_shape,
        scratch_shapes=[pltpu.VMEM(shape, jnp.float32) for shape in scratch],
        compiler_params=pltpu.CompilerParams(vmem_limit_bytes=32 * 2**20),
        cost_estimate=cost(flops, 2**20),
        name=name,
    )(*args)


def three(left, right, dims):
    def one(a, b):
        return lax.dot_general(a, b, (dims, ((), ())), preferred_element_type=jnp.float32)

    return one(left[0], right[1]) + one(left[1], right[0]) + one(left[0], right[0])


def products_kernel(x_ref, r_ref, p_ref, a_ref, b_ref, out_ref, panel_ref):
    k = x_ref.shape[0]
    wide = 3 * k

    @pl.when(pl.program_id(0) == 0)
    def _():
        for i, ref in enumerate((x_ref, r_ref, p_ref)):
            high, low = split(ref[...])
            panel_ref[i * k : (i + 1) * k] = high
            panel_ref[wide + i * k : wide + (i + 1) * k] = low

    def one(a, b):
        return jnp.dot(a, b, preferred_element_type=jnp.float32)

    for at, ref in ((0, a_ref), (wide, b_ref)):
        high, low = split(ref[...])
        both = one(panel_ref[...], high)
        prod = both[:wide] + both[wide:] + one(panel_ref[:wide], low)
        for i in range(out_ref.shape[0]):
            lanes = out_ref.shape[2]
            out_ref[i, at : at + wide] = prod[:, i * lanes : (i + 1) * lanes]


def gram_kernel(parts_ref, panel_ref, prods_ref, out_ref):
    wide = panel_ref.shape[0]
    k = wide // 3
    prods = parts_ref[0]
    for i in range(1, parts_ref.shape[0]):
        prods = prods + parts_ref[i]
    prods_ref[...] = prods
    gram = three(split(prods), split(panel_ref[...]), NT)
    at = 0
    for i in range(3):
        for j in range(i + 1):
            pair = []
            for base in (0, wide):
                block = gram[base + i * k : base + (i + 1) * k, j * k : (j + 1) * k]
                other = gram[base + j * k : base + (j + 1) * k, i * k : (i + 1) * k]
                pair.append(0.5 * (block + other.T))
            out_ref[at : at + k] = jnp.concatenate(pair, 1)
            at += k


def tests_kernel(turn_ref, prods_ref, basis_ref, own_ref, out_ref, resid_ref):
    k = turn_ref.shape[1]
    resid = dot(turn_ref[...], prods_ref[...], TN)
    resid_ref[:k] = resid
    resid_ref[k:] = jnp.zeros_like(resid)
    kept = dot(basis_ref[...], own_ref[...], TN)
    out_ref[:k] = kept[:k]
    out_ref[k : 2 * k] = resid
    out_ref[2 * k :] = kept[k:]


def fresh_kernel(parts_ref, tests_ref, more_ref, out_ref):
    more = parts_ref[0]
    for i in range(1, parts_ref.shape[0]):
        more = more + parts_ref[i]
    more_ref[...] = more
    out_ref[...] = three(split(tests_ref[...]), split(more), ((1,), (0,)))


def outputs_kernel(mix_ref, x_ref, r_ref, p_ref, resid_ref, x_out, p_out):
    k = x_ref.shape[0]
    resid = jnp.concatenate([resid_ref[i] for i in range(resid_ref.shape[0])], 1)
    vectors = jnp.concatenate([x_ref[...], r_ref[...], p_ref[...], resid], 0)
    out = three(split(mix_ref[...]), split(vectors), TN)
    x_out[...] = out[:k]
    p_out[...] = out[k:]


def products(x, r, p, a, b, pieces):
    k, rows = x.shape
    lanes = a.shape[1] // pieces
    each = 2
    block = pl.BlockSpec((k, rows), lambda i: (0, 0))
    tile = pl.BlockSpec((rows, each * lanes), lambda i: (0, i))
    return pl.pallas_call(
        products_kernel,
        grid=(pieces // each,),
        in_specs=[block, block, block, tile, tile],
        out_specs=pl.BlockSpec((each, 6 * k, lanes), lambda i: (i, 0, 0)),
        out_shape=f32(pieces, 6 * k, lanes),
        scratch_shapes=[pltpu.VMEM((6 * k, rows), jnp.bfloat16)],
        compiler_params=pltpu.CompilerParams(vmem_limit_bytes=60 * 2**20),
        cost_estimate=cost(1e10, 8 * rows * a.shape[1]),
        name="products",
    )(x, r, p, a, b)


def first_step(k, order, packed, prods, a, b):
    rows, cols = a.shape
    inside = pl.BlockSpec(memory_space=pltpu.VMEM)
    outside = pl.BlockSpec(memory_space=pl.ANY)
    return pl.pallas_call(
        functools.partial(first_kernel, k, order),
        in_specs=[inside, inside, outside, outside],
        out_specs=(inside, inside, inside),
        out_shape=(f32(6 * k, k), f32(3 * k, 2 * k), f32(rows, 2 * k)),
        scratch_shapes=[pltpu.VMEM((3 * k, 3 * k), jnp.float32)] * 2
        + [pltpu.VMEM((rows, cols), jnp.float32)] * 2
        + [pltpu.VMEM((cols, 2 * k), jnp.bfloat16)] * 2
        + [pltpu.SemaphoreType.DMA((2,))],
        compiler_params=pltpu.CompilerParams(vmem_limit_bytes=56 * 2**20),
        cost_estimate=cost(1.7e10, 8 * rows * cols),
        name="first_step",
    )(packed, prods, a, b)


def outputs(mix, x, r, p, resid):
    k, rows = x.shape
    pieces, _, lanes = resid.shape
    each = 8
    part = pl.BlockSpec((k, each * lanes), lambda i: (0, i))
    return pl.pallas_call(
        outputs_kernel,
        grid=(pieces // each,),
        in_specs=[
            pl.BlockSpec(mix.shape, lambda i: (0, 0)),
            part,
            part,
            part,
            pl.BlockSpec((each, k, lanes), lambda i: (i, 0, 0)),
        ],
        out_specs=(part, part),
        out_shape=(f32(k, rows), f32(k, rows)),
        compiler_params=pltpu.CompilerParams(vmem_limit_bytes=60 * 2**20),
        cost_estimate=cost(3e9, 40 * rows * k),
        name="outputs",
    )(mix, x, r, p, resid)


def local(a_matrix, b_matrix, x_block, r_block, p_block):
    rows, cols = lax.axis_size("row"), lax.axis_size("col")
    count = rows * cols
    k = x_block.shape[1]
    order = x_block.shape[0] * rows
    piece = order // count
    to_col = [(b, (b % rows) * cols + b // rows) for b in range(count)]
    to_row = [(d, s) for s, d in to_col]

    panel = [x_block.T, r_block.T, p_block.T]
    start = lax.axis_index("col") * piece
    own_row = jnp.concatenate(
        [lax.dynamic_slice_in_dim(x, start, piece, 1) for x in panel], 0
    )
    own_col = lax.ppermute(own_row, BOTH, to_col)

    prods = products(*panel, a_matrix, b_matrix, rows)
    prods = lax.all_to_all(prods, "row", 0, 0)
    prod_col, packed = call(
        gram_kernel, "gram", (f32(6 * k, piece), f32(6 * k, 2 * k)), [], 2e9, prods, own_col
    )
    prod_row = lax.ppermute(prod_col, BOTH, to_row)
    prods_col = lax.all_gather(prod_col, "row")
    packed = sum_everywhere(packed)
    turn, basis, parts = first_step(k, order, packed, prods_col, a_matrix, b_matrix)
    turn, prod_row, parts = lax.optimization_barrier((turn, prod_row, parts))
    parts = lax.all_to_all(parts.reshape(cols, piece, 2 * k), "col", 0, 0)
    old = call(kept_kernel, "kept", f32(4 * k, 2 * k), [(3 * k, 3 * k)], 3e9, packed, basis)
    tests, resid_row = call(
        tests_kernel,
        "tests",
        (f32(3 * k, piece), f32(2 * k, piece)),
        [],
        1e9,
        turn,
        prod_row,
        basis,
        own_row,
    )
    more_row, fresh = call(
        fresh_kernel, "fresh", (f32(piece, 2 * k), f32(3 * k, 2 * k)), [], 1e9, parts, tests
    )
    fresh, resid_row = lax.optimization_barrier((fresh, resid_row))
    resid = lax.all_gather(resid_row, "col")
    fresh = sum_everywhere(fresh)
    r_own, mix = call(
        functools.partial(second_kernel, k, order),
        "ritz_second",
        (f32(cols, k, piece), f32(4 * k, 2 * k)),
        [(3 * k, 3 * k)] * 2,
        1e7,
        old,
        fresh,
        basis,
        prod_row,
        more_row,
    )
    r_next = lax.all_to_all(r_own, "col", 0, 0)
    x_next, p_next = outputs(mix, *panel, resid)
    r_next, x_next, p_next = lax.optimization_barrier((r_next, x_next, p_next))
    r_next = r_next.transpose(1, 0, 2).reshape(k, -1)
    return (x_next.T, r_next.T, p_next.T)


def solution(mesh):
    return jax.shard_map(
        local,
        mesh=mesh,
        in_specs=(P("row", "col"), P("row", "col"), P("row", None), P("row", None), P("row", None)),
        out_specs=(P("row", None), P("row", None), P("row", None)),
        check_vma=False,
    )
```

```python
import functools
import math

import jax
import jax.numpy as jnp
from jax import lax
from jax.experimental import pallas as pl
from jax.experimental.pallas import tpu as pltpu
from jax.sharding import PartitionSpec as P

NS_STEPS = 8
BOTH = ("row", "col")


def mm(left, right, dims=((1,), (0,)), precision=lax.Precision.HIGHEST):
    return lax.dot_general(
        left, right, (dims, ((), ())), precision=precision, preferred_element_type=jnp.float32
    )


def share(x, axis):
    copies = jnp.broadcast_to(x[None], (lax.axis_size(axis),) + x.shape)
    return lax.all_to_all(copies, axis, 0, 0)


def sum_everywhere(x):
    parts = x.reshape(lax.axis_size("row"), -1, x.shape[-1])
    own = lax.all_to_all(parts, "row", 0, 0).sum(0)
    own = share(own, "col").sum(0)
    return share(own, "row").reshape(x.shape)


def dot(left, right, dims=((1,), (0,))):
    return lax.dot_general(
        left, right, (dims, ((), ())),
        precision=lax.Precision.HIGHEST, preferred_element_type=jnp.float32,
    )


NT = ((1,), (1,))
TN = ((0,), (0,))


def split(x):
    high = x.astype(jnp.bfloat16)
    return high, (x - high.astype(jnp.float32)).astype(jnp.bfloat16)


def dot3(left, right):
    def one(a, b):
        return jnp.dot(a, b, preferred_element_type=jnp.float32)

    return one(left[0], right[1]) + one(left[1], right[0]) + one(left[0], right[0])


def inverse_factor(block):
    k = block.shape[0]
    height = 8
    diag = lax.broadcasted_iota(jnp.int32, (k, k), 0) == lax.broadcasted_iota(jnp.int32, (k, k), 1)
    wide = jnp.concatenate([block, diag.astype(jnp.float32)], 1)
    full = (height, 2 * k)
    strips = [wide[i : i + height] for i in range(0, k, height)]
    line = lax.broadcasted_iota(jnp.int32, full, 0)
    done = []
    for at in range(k // height):
        first = at * height
        rows = [jnp.broadcast_to(strips[at][i : i + 1], full) for i in range(height)]
        elem = [
            [jnp.broadcast_to(rows[m][:, first + i : first + i + 1], full) for i in range(m + 1)]
            for m in range(height)
        ]
        later = range(at + 1, k // height)
        cols = {
            t: [
                jnp.broadcast_to(strips[t][:, first + i : first + i + 1], full)
                for i in range(height)
            ]
            for t in later
        }
        low = [[None] * height for _ in range(height)]
        inv = {}
        out = None
        for i in range(0, height, 2):
            a, b, c = elem[i][i], elem[i + 1][i], elem[i + 1][i + 1]
            det = a * c - b * b
            inv[i] = 1.0 / det
            for m in range(i + 2, height):
                u, v = elem[m][i], elem[m][i + 1]
                low[m][i] = (u * c - v * b) * inv[i]
                low[m][i + 1] = (v * a - u * b) * inv[i]
                for n in range(i + 2, m + 1):
                    elem[m][n] = elem[m][n] - (
                        low[m][i] * elem[n][i] + low[m][i + 1] * elem[n][i + 1]
                    )
                rows[m] = rows[m] - (low[m][i] * rows[i] + low[m][i + 1] * rows[i + 1])
            scale = 1.0 / a
            upper = rows[i] * (1.0 / jnp.sqrt(a))
            lower = (rows[i + 1] - (b * scale) * rows[i]) * (1.0 / jnp.sqrt(det * scale))
            out = upper if out is None else jnp.where(line == i, upper, out)
            out = jnp.where(line == i + 1, lower, out)
        done.append(out)
        if not later:
            break
        solved = [None] * height
        for i in reversed(range(0, height, 2)):
            a, b, c = elem[i][i], elem[i + 1][i], elem[i + 1][i + 1]
            solved[i] = (c * rows[i] - b * rows[i + 1]) * inv[i]
            solved[i + 1] = (a * rows[i + 1] - b * rows[i]) * inv[i]
            for m in range(i + 2, height):
                solved[i] = solved[i] - low[m][i] * solved[m]
                solved[i + 1] = solved[i + 1] - low[m][i + 1] * solved[m]
        for t in later:
            for m in range(height):
                strips[t] = strips[t] - cols[t][m] * solved[m]
    return jnp.concatenate(done, 0)[:, k:]


def ritz_step(k, order, blocks_b, whole_a, inv_ref):
    b00, b10, b11, b20, b21, b22 = blocks_b
    t0 = inverse_factor(b00)
    l10 = dot(b10, t0, NT)
    l20 = dot(b20, t0, NT)
    t1 = inverse_factor(b11 - dot(l10, l10, NT))
    l21 = dot(b21 - dot(l20, l10, NT), t1, NT)
    t2 = inverse_factor(b22 - dot(l20, l20, NT) - dot(l21, l21, NT))
    t10 = -dot(t1, dot(l10, t0))
    t20 = -dot(t2, dot(l20, t0) + dot(l21, t10))
    t21 = -dot(t2, dot(l21, t1))
    inv_ref[...] = jnp.zeros_like(inv_ref)
    inv_ref[:k, :k] = t0
    inv_ref[k : 2 * k, :k] = t10
    inv_ref[k : 2 * k, k : 2 * k] = t1
    inv_ref[2 * k :, : 2 * k] = jnp.concatenate([t20, t21], 1)
    inv_ref[2 * k :, 2 * k :] = t2
    inverse = inv_ref[...]
    middle = dot(dot(inverse, whole_a), inverse, NT)
    middle = 0.5 * (middle + middle.T)
    size = 3 * k
    diag = lax.broadcasted_iota(jnp.int32, (size, size), 0) == lax.broadcasted_iota(
        jnp.int32, (size, size), 1
    )

    def total(x):
        return jnp.sum(jnp.sum(x, 0, keepdims=True), 1, keepdims=True)

    shift = total(jnp.where(diag, middle, 0.0)) * (1.0 / size)
    sign = middle - jnp.where(diag, shift, 0.0)
    sign = sign * (1.0 / jnp.sqrt(total(sign * sign) + 1e-06))
    for turn in range(NS_STEPS - 1):
        parts = split(sign)
        sign = 1.5 * sign - 0.5 * dot3(parts, split(dot3(parts, parts)))
    parts, first = split(sign), sign[:, :k]
    first = 1.5 * first - 0.5 * dot3(parts, split(dot3(parts, split(first))))
    filtered = 0.5 * (jnp.where(diag[:, :k], 1.0, 0.0) - first)
    coords = dot(inverse, filtered, TN) * math.sqrt(order)
    reduced = dot(filtered, dot(middle, filtered), TN)
    return coords, reduced


def put_whole(ref, blocks, k):
    b00, b10, b11, b20, b21, b22 = blocks
    ref[:k, : 2 * k] = jnp.concatenate([b00, b10.T], 1)
    ref[:k, 2 * k :] = b20.T
    ref[k : 2 * k, : 2 * k] = jnp.concatenate([b10, b11], 1)
    ref[k : 2 * k, 2 * k :] = b21.T
    ref[2 * k :, : 2 * k] = jnp.concatenate([b20, b21], 1)
    ref[2 * k :, 2 * k :] = b22
    return ref[...]


def first_kernel(
    k,
    order,
    packed_ref,
    prods_ref,
    a_hbm,
    b_hbm,
    turn_ref,
    basis_ref,
    out_ref,
    inv_ref,
    whole_ref,
    a_ref,
    b_ref,
    high_ref,
    low_ref,
    sems,
):
    copies = [
        pltpu.make_async_copy(a_hbm, a_ref, sems.at[0]),
        pltpu.make_async_copy(b_hbm, b_ref, sems.at[1]),
    ]
    for copy in copies:
        copy.start()
    blocks = [packed_ref[i * k : (i + 1) * k] for i in range(6)]
    whole_a = put_whole(whole_ref, [x[:, :k] for x in blocks], k)
    coords, reduced = ritz_step(k, order, [x[:, k:] for x in blocks], whole_a, inv_ref)
    turn_ref[: 3 * k] = coords
    turn_ref[3 * k :] = -dot(coords, reduced)
    basis_ref[:k] = jnp.concatenate([coords[:k], jnp.zeros((k, k), jnp.float32)], 1)
    basis_ref[k:] = jnp.concatenate([coords[k:], coords[k:]], 1)

    pieces, _, lanes = prods_ref.shape
    turn = split(turn_ref[...])
    for i in range(pieces):
        block = three(turn, split(prods_ref[i]), TN).T
        high = block.astype(jnp.bfloat16).astype(jnp.float32)
        low = block - high
        high_ref[i * lanes : (i + 1) * lanes] = jnp.concatenate([high, low], 1).astype(jnp.bfloat16)
        low_ref[i * lanes : (i + 1) * lanes] = jnp.concatenate([low, high], 1).astype(jnp.bfloat16)
    for copy in copies:
        copy.wait()
    height = 256
    lane = lax.broadcasted_iota(jnp.int32, (height, 2 * k), 1)

    @pl.loop(0, out_ref.shape[0] // height, unroll=8)
    def _(step):
        rows = pl.ds(pl.multiple_of(step * height, height), height)
        sums = []
        for ref, parts_ref in ((a_ref, high_ref), (b_ref, low_ref)):
            high, low = split(ref[rows, :])
            part = jnp.dot(high, parts_ref[...], preferred_element_type=jnp.float32) + jnp.dot(
                low, parts_ref[...], preferred_element_type=jnp.float32
            )
            sums.append(part + pltpu.roll(part, k, 1))
        out_ref[rows, :] = jnp.where(lane < k, sums[0], sums[1])


def kept_kernel(packed_ref, basis_ref, old_ref, whole_ref):
    k = basis_ref.shape[1] // 2
    blocks = [packed_ref[i * k : (i + 1) * k] for i in range(6)]
    basis = basis_ref[...]
    for i in range(2):
        whole = put_whole(whole_ref, [x[:, i * k : (i + 1) * k] for x in blocks], k)
        old_ref[i * 2 * k : (i + 1) * 2 * k] = dot(basis, dot(whole, basis), TN)


def second_kernel(
    k,
    order,
    old_ref,
    fresh_ref,
    basis_ref,
    prod_ref,
    more_ref,
    r_ref,
    mix_ref,
    inv_ref,
    a_ref,
):
    def blocks(old, new):
        mid = new[k : 2 * k]
        return [
            old[:k, :k],
            new[:k].T,
            0.5 * (mid + mid.T),
            old[k:, :k],
            new[2 * k :],
            old[k:, k:],
        ]

    whole_a = put_whole(a_ref, blocks(old_ref[: 2 * k], fresh_ref[:, :k]), k)
    blocks_b = blocks(old_ref[2 * k :], fresh_ref[:, k:])
    coords, reduced = ritz_step(k, order, blocks_b, whole_a, inv_ref)
    basis = basis_ref[...]
    from_r = coords[k : 2 * k]
    move_p = dot(basis[:, k:], coords[2 * k :])
    move_x = dot(basis, jnp.concatenate([coords[:k], coords[2 * k :]], 0))
    more = more_ref[...].T
    mix_ref[: 3 * k] = jnp.concatenate([move_x, move_p], 1)
    mix_ref[3 * k :] = jnp.concatenate([from_r, from_r], 1)
    weights = jnp.concatenate(
        [move_x, -dot(move_x, reduced), from_r, -dot(from_r, reduced)], 0
    )
    vectors = jnp.concatenate([prod_ref[...], more], 0)
    resid = three(split(weights), split(vectors), TN)
    for i in range(r_ref.shape[0]):
        r_ref[i] = resid


def f32(*shape):
    return jax.ShapeDtypeStruct(shape, jnp.float32)


def cost(flops, size):
    return pl.CostEstimate(flops=int(flops), bytes_accessed=int(size), transcendentals=0)


def call(kernel, name, out_shape, scratch, flops, *args):
    return pl.pallas_call(
        kernel,
        out_shape=out_shape,
        scratch_shapes=[pltpu.VMEM(shape, jnp.float32) for shape in scratch],
        compiler_params=pltpu.CompilerParams(vmem_limit_bytes=32 * 2**20),
        cost_estimate=cost(flops, 2**20),
        name=name,
    )(*args)


def three(left, right, dims):
    def one(a, b):
        return lax.dot_general(a, b, (dims, ((), ())), preferred_element_type=jnp.float32)

    return one(left[0], right[1]) + one(left[1], right[0]) + one(left[0], right[0])


def products_kernel(x_ref, r_ref, p_ref, a_ref, b_ref, out_ref, panel_ref):
    k = x_ref.shape[0]
    wide = 3 * k

    @pl.when(pl.program_id(0) == 0)
    def _():
        for i, ref in enumerate((x_ref, r_ref, p_ref)):
            high, low = split(ref[...])
            panel_ref[i * k : (i + 1) * k] = high
            panel_ref[wide + i * k : wide + (i + 1) * k] = low

    def one(a, b):
        return jnp.dot(a, b, preferred_element_type=jnp.float32)

    for at, ref in ((0, a_ref), (wide, b_ref)):
        high, low = split(ref[...])
        both = one(panel_ref[...], high)
        prod = both[:wide] + both[wide:] + one(panel_ref[:wide], low)
        for i in range(out_ref.shape[0]):
            lanes = out_ref.shape[2]
            out_ref[i, at : at + wide] = prod[:, i * lanes : (i + 1) * lanes]


def gram_kernel(parts_ref, panel_ref, prods_ref, out_ref):
    wide = panel_ref.shape[0]
    k = wide // 3
    prods = parts_ref[0]
    for i in range(1, parts_ref.shape[0]):
        prods = prods + parts_ref[i]
    prods_ref[...] = prods
    gram = three(split(prods), split(panel_ref[...]), NT)
    at = 0
    for i in range(3):
        for j in range(i + 1):
            pair = []
            for base in (0, wide):
                block = gram[base + i * k : base + (i + 1) * k, j * k : (j + 1) * k]
                other = gram[base + j * k : base + (j + 1) * k, i * k : (i + 1) * k]
                pair.append(0.5 * (block + other.T))
            out_ref[at : at + k] = jnp.concatenate(pair, 1)
            at += k


def tests_kernel(turn_ref, prods_ref, basis_ref, own_ref, out_ref, resid_ref):
    k = turn_ref.shape[1]
    resid = dot(turn_ref[...], prods_ref[...], TN)
    resid_ref[:k] = resid
    resid_ref[k:] = jnp.zeros_like(resid)
    kept = dot(basis_ref[...], own_ref[...], TN)
    out_ref[:k] = kept[:k]
    out_ref[k : 2 * k] = resid
    out_ref[2 * k :] = kept[k:]


def fresh_kernel(parts_ref, tests_ref, more_ref, out_ref):
    more = parts_ref[0]
    for i in range(1, parts_ref.shape[0]):
        more = more + parts_ref[i]
    more_ref[...] = more
    out_ref[...] = three(split(tests_ref[...]), split(more), ((1,), (0,)))


def outputs_kernel(mix_ref, x_ref, r_ref, p_ref, resid_ref, x_out, p_out):
    k = x_ref.shape[0]
    resid = jnp.concatenate([resid_ref[i] for i in range(resid_ref.shape[0])], 1)
    vectors = jnp.concatenate([x_ref[...], r_ref[...], p_ref[...], resid], 0)
    out = three(split(mix_ref[...]), split(vectors), TN)
    x_out[...] = out[:k]
    p_out[...] = out[k:]


def products(x, r, p, a, b, pieces):
    k, rows = x.shape
    lanes = a.shape[1] // pieces
    each = 2
    block = pl.BlockSpec((k, rows), lambda i: (0, 0))
    tile = pl.BlockSpec((rows, each * lanes), lambda i: (0, i))
    return pl.pallas_call(
        products_kernel,
        grid=(pieces // each,),
        in_specs=[block, block, block, tile, tile],
        out_specs=pl.BlockSpec((each, 6 * k, lanes), lambda i: (i, 0, 0)),
        out_shape=f32(pieces, 6 * k, lanes),
        scratch_shapes=[pltpu.VMEM((6 * k, rows), jnp.bfloat16)],
        compiler_params=pltpu.CompilerParams(vmem_limit_bytes=60 * 2**20),
        cost_estimate=cost(1e10, 8 * rows * a.shape[1]),
        name="products",
    )(x, r, p, a, b)


def first_step(k, order, packed, prods, a, b):
    rows, cols = a.shape
    inside = pl.BlockSpec(memory_space=pltpu.VMEM)
    outside = pl.BlockSpec(memory_space=pl.ANY)
    return pl.pallas_call(
        functools.partial(first_kernel, k, order),
        in_specs=[inside, inside, outside, outside],
        out_specs=(inside, inside, inside),
        out_shape=(f32(6 * k, k), f32(3 * k, 2 * k), f32(rows, 2 * k)),
        scratch_shapes=[pltpu.VMEM((3 * k, 3 * k), jnp.float32)] * 2
        + [pltpu.VMEM((rows, cols), jnp.float32)] * 2
        + [pltpu.VMEM((cols, 2 * k), jnp.bfloat16)] * 2
        + [pltpu.SemaphoreType.DMA((2,))],
        compiler_params=pltpu.CompilerParams(vmem_limit_bytes=56 * 2**20),
        cost_estimate=cost(1.7e10, 8 * rows * cols),
        name="first_step",
    )(packed, prods, a, b)


def outputs(mix, x, r, p, resid):
    k, rows = x.shape
    pieces, _, lanes = resid.shape
    each = 8
    part = pl.BlockSpec((k, each * lanes), lambda i: (0, i))
    return pl.pallas_call(
        outputs_kernel,
        grid=(pieces // each,),
        in_specs=[
            pl.BlockSpec(mix.shape, lambda i: (0, 0)),
            part,
            part,
            part,
            pl.BlockSpec((each, k, lanes), lambda i: (i, 0, 0)),
        ],
        out_specs=(part, part),
        out_shape=(f32(k, rows), f32(k, rows)),
        compiler_params=pltpu.CompilerParams(vmem_limit_bytes=16 * 2**20),
        cost_estimate=cost(3e9, 40 * rows * k),
        name="outputs",
    )(mix, x, r, p, resid)


def local(a_matrix, b_matrix, x_block, r_block, p_block):
    rows, cols = lax.axis_size("row"), lax.axis_size("col")
    count = rows * cols
    k = x_block.shape[1]
    order = x_block.shape[0] * rows
    piece = order // count
    to_col = [(b, (b % rows) * cols + b // rows) for b in range(count)]
    to_row = [(d, s) for s, d in to_col]

    panel = [x_block.T, r_block.T, p_block.T]
    start = lax.axis_index("col") * piece
    own_row = jnp.concatenate(
        [lax.dynamic_slice_in_dim(x, start, piece, 1) for x in panel], 0
    )
    own_col = lax.ppermute(own_row, BOTH, to_col)

    prods = products(*panel, a_matrix, b_matrix, rows)
    prods = lax.all_to_all(prods, "row", 0, 0)
    prod_col, packed = call(
        gram_kernel, "gram", (f32(6 * k, piece), f32(6 * k, 2 * k)), [], 2e9, prods, own_col
    )
    prod_row = lax.ppermute(prod_col, BOTH, to_row)
    prods_col = lax.all_gather(prod_col, "row")
    packed = sum_everywhere(packed)
    turn, basis, parts = first_step(k, order, packed, prods_col, a_matrix, b_matrix)
    turn, prod_row, parts = lax.optimization_barrier((turn, prod_row, parts))
    parts = lax.all_to_all(parts.reshape(cols, piece, 2 * k), "col", 0, 0)
    old = call(kept_kernel, "kept", f32(4 * k, 2 * k), [(3 * k, 3 * k)], 3e9, packed, basis)
    tests, resid_row = call(
        tests_kernel,
        "tests",
        (f32(3 * k, piece), f32(2 * k, piece)),
        [],
        1e9,
        turn,
        prod_row,
        basis,
        own_row,
    )
    more_row, fresh = call(
        fresh_kernel, "fresh", (f32(piece, 2 * k), f32(3 * k, 2 * k)), [], 1e9, parts, tests
    )
    fresh, resid_row = lax.optimization_barrier((fresh, resid_row))
    resid = lax.all_gather(resid_row, "col")
    fresh = sum_everywhere(fresh)
    r_own, mix = call(
        functools.partial(second_kernel, k, order),
        "ritz_second",
        (f32(cols, k, piece), f32(4 * k, 2 * k)),
        [(3 * k, 3 * k)] * 2,
        1e7,
        old,
        fresh,
        basis,
        prod_row,
        more_row,
    )
    r_next = lax.all_to_all(r_own, "col", 0, 0)
    x_next, p_next = outputs(mix, *panel, resid)
    r_next, x_next, p_next = lax.optimization_barrier((r_next, x_next, p_next))
    r_next = r_next.transpose(1, 0, 2).reshape(k, -1)
    return (x_next.T, r_next.T, p_next.T)


def solution(mesh):
    return jax.shard_map(
        local,
        mesh=mesh,
        in_specs=(P("row", "col"), P("row", "col"), P("row", None), P("row", None), P("row", None)),
        out_specs=(P("row", None), P("row", None), P("row", None)),
        check_vma=False,
    )
```

```python
import functools
import math

import jax
import jax.numpy as jnp
from jax import lax
from jax.experimental import pallas as pl
from jax.experimental.pallas import tpu as pltpu
from jax.sharding import PartitionSpec as P

NS_STEPS = 8
BOTH = ("row", "col")


def mm(left, right, dims=((1,), (0,)), precision=lax.Precision.HIGHEST):
    return lax.dot_general(
        left, right, (dims, ((), ())), precision=precision, preferred_element_type=jnp.float32
    )


def share(x, axis):
    copies = jnp.broadcast_to(x[None], (lax.axis_size(axis),) + x.shape)
    return lax.all_to_all(copies, axis, 0, 0)


def sum_everywhere(x):
    parts = x.reshape(lax.axis_size("row"), -1, x.shape[-1])
    own = lax.all_to_all(parts, "row", 0, 0).sum(0)
    own = share(own, "col").sum(0)
    return share(own, "row").reshape(x.shape)


def dot(left, right, dims=((1,), (0,))):
    return lax.dot_general(
        left, right, (dims, ((), ())),
        precision=lax.Precision.HIGHEST, preferred_element_type=jnp.float32,
    )


NT = ((1,), (1,))
TN = ((0,), (0,))


def split(x):
    high = x.astype(jnp.bfloat16)
    return high, (x - high.astype(jnp.float32)).astype(jnp.bfloat16)


def dot3(left, right):
    def one(a, b):
        return jnp.dot(a, b, preferred_element_type=jnp.float32)

    return one(left[0], right[1]) + one(left[1], right[0]) + one(left[0], right[0])


def inverse_factor(block):
    k = block.shape[0]
    height = 8
    diag = lax.broadcasted_iota(jnp.int32, (k, k), 0) == lax.broadcasted_iota(jnp.int32, (k, k), 1)
    wide = jnp.concatenate([block, diag.astype(jnp.float32)], 1)
    full = (height, 2 * k)
    strips = [wide[i : i + height] for i in range(0, k, height)]
    line = lax.broadcasted_iota(jnp.int32, full, 0)
    done = []
    for at in range(k // height):
        first = at * height
        rows = [jnp.broadcast_to(strips[at][i : i + 1], full) for i in range(height)]
        elem = [
            [jnp.broadcast_to(rows[m][:, first + i : first + i + 1], full) for i in range(m + 1)]
            for m in range(height)
        ]
        later = range(at + 1, k // height)
        cols = {
            t: [
                jnp.broadcast_to(strips[t][:, first + i : first + i + 1], full)
                for i in range(height)
            ]
            for t in later
        }
        low = [[None] * height for _ in range(height)]
        inv = {}
        out = None
        for i in range(0, height, 2):
            a, b, c = elem[i][i], elem[i + 1][i], elem[i + 1][i + 1]
            det = a * c - b * b
            inv[i] = 1.0 / det
            for m in range(i + 2, height):
                u, v = elem[m][i], elem[m][i + 1]
                low[m][i] = (u * c - v * b) * inv[i]
                low[m][i + 1] = (v * a - u * b) * inv[i]
                for n in range(i + 2, m + 1):
                    elem[m][n] = elem[m][n] - (
                        low[m][i] * elem[n][i] + low[m][i + 1] * elem[n][i + 1]
                    )
                rows[m] = rows[m] - (low[m][i] * rows[i] + low[m][i + 1] * rows[i + 1])
            scale = 1.0 / a
            upper = rows[i] * (1.0 / jnp.sqrt(a))
            lower = (rows[i + 1] - (b * scale) * rows[i]) * (1.0 / jnp.sqrt(det * scale))
            out = upper if out is None else jnp.where(line == i, upper, out)
            out = jnp.where(line == i + 1, lower, out)
        done.append(out)
        if not later:
            break
        solved = [None] * height
        for i in reversed(range(0, height, 2)):
            a, b, c = elem[i][i], elem[i + 1][i], elem[i + 1][i + 1]
            solved[i] = (c * rows[i] - b * rows[i + 1]) * inv[i]
            solved[i + 1] = (a * rows[i + 1] - b * rows[i]) * inv[i]
            for m in range(i + 2, height):
                solved[i] = solved[i] - low[m][i] * solved[m]
                solved[i + 1] = solved[i + 1] - low[m][i + 1] * solved[m]
        for t in later:
            for m in range(height):
                strips[t] = strips[t] - cols[t][m] * solved[m]
    return jnp.concatenate(done, 0)[:, k:]


def ritz_step(k, order, blocks_b, whole_a, inv_ref):
    b00, b10, b11, b20, b21, b22 = blocks_b
    t0 = inverse_factor(b00)
    l10 = dot(b10, t0, NT)
    l20 = dot(b20, t0, NT)
    t1 = inverse_factor(b11 - dot(l10, l10, NT))
    l21 = dot(b21 - dot(l20, l10, NT), t1, NT)
    t2 = inverse_factor(b22 - dot(l20, l20, NT) - dot(l21, l21, NT))
    t10 = -dot(t1, dot(l10, t0))
    t20 = -dot(t2, dot(l20, t0) + dot(l21, t10))
    t21 = -dot(t2, dot(l21, t1))
    inv_ref[...] = jnp.zeros_like(inv_ref)
    inv_ref[:k, :k] = t0
    inv_ref[k : 2 * k, :k] = t10
    inv_ref[k : 2 * k, k : 2 * k] = t1
    inv_ref[2 * k :, : 2 * k] = jnp.concatenate([t20, t21], 1)
    inv_ref[2 * k :, 2 * k :] = t2
    inverse = inv_ref[...]
    middle = dot(dot(inverse, whole_a), inverse, NT)
    middle = 0.5 * (middle + middle.T)
    size = 3 * k
    diag = lax.broadcasted_iota(jnp.int32, (size, size), 0) == lax.broadcasted_iota(
        jnp.int32, (size, size), 1
    )

    def total(x):
        return jnp.sum(jnp.sum(x, 0, keepdims=True), 1, keepdims=True)

    shift = total(jnp.where(diag, middle, 0.0)) * (1.0 / size)
    sign = middle - jnp.where(diag, shift, 0.0)
    sign = sign * (1.0 / jnp.sqrt(total(sign * sign) + 1e-06))
    for turn in range(NS_STEPS - 1):
        parts = split(sign)
        sign = 1.5 * sign - 0.5 * dot3(parts, split(dot3(parts, parts)))
    parts, first = split(sign), sign[:, :k]
    first = 1.5 * first - 0.5 * dot3(parts, split(dot3(parts, split(first))))
    filtered = 0.5 * (jnp.where(diag[:, :k], 1.0, 0.0) - first)
    coords = dot(inverse, filtered, TN) * math.sqrt(order)
    reduced = dot(filtered, dot(middle, filtered), TN)
    return coords, reduced


def put_whole(ref, blocks, k):
    b00, b10, b11, b20, b21, b22 = blocks
    ref[:k, : 2 * k] = jnp.concatenate([b00, b10.T], 1)
    ref[:k, 2 * k :] = b20.T
    ref[k : 2 * k, : 2 * k] = jnp.concatenate([b10, b11], 1)
    ref[k : 2 * k, 2 * k :] = b21.T
    ref[2 * k :, : 2 * k] = jnp.concatenate([b20, b21], 1)
    ref[2 * k :, 2 * k :] = b22
    return ref[...]


def first_kernel(
    k,
    order,
    packed_ref,
    prods_ref,
    a_hbm,
    b_hbm,
    turn_ref,
    basis_ref,
    out_ref,
    inv_ref,
    whole_ref,
    a_ref,
    b_ref,
    high_ref,
    low_ref,
    sems,
):
    copies = [
        pltpu.make_async_copy(a_hbm, a_ref, sems.at[0]),
        pltpu.make_async_copy(b_hbm, b_ref, sems.at[1]),
    ]
    for copy in copies:
        copy.start()
    blocks = [packed_ref[i * k : (i + 1) * k] for i in range(6)]
    whole_a = put_whole(whole_ref, [x[:, :k] for x in blocks], k)
    coords, reduced = ritz_step(k, order, [x[:, k:] for x in blocks], whole_a, inv_ref)
    turn_ref[: 3 * k] = coords
    turn_ref[3 * k :] = -dot(coords, reduced)
    basis_ref[:k] = jnp.concatenate([coords[:k], jnp.zeros((k, k), jnp.float32)], 1)
    basis_ref[k:] = jnp.concatenate([coords[k:], coords[k:]], 1)

    pieces, _, lanes = prods_ref.shape
    turn = split(turn_ref[...])
    for i in range(pieces):
        block = three(turn, split(prods_ref[i]), TN).T
        high = block.astype(jnp.bfloat16).astype(jnp.float32)
        low = block - high
        high_ref[i * lanes : (i + 1) * lanes] = jnp.concatenate([high, low], 1).astype(jnp.bfloat16)
        low_ref[i * lanes : (i + 1) * lanes] = jnp.concatenate([low, high], 1).astype(jnp.bfloat16)
    for copy in copies:
        copy.wait()
    height = 256
    lane = lax.broadcasted_iota(jnp.int32, (height, 2 * k), 1)

    @pl.loop(0, out_ref.shape[0] // height, unroll=8)
    def _(step):
        rows = pl.ds(pl.multiple_of(step * height, height), height)
        sums = []
        for ref, parts_ref in ((a_ref, high_ref), (b_ref, low_ref)):
            high, low = split(ref[rows, :])
            part = jnp.dot(high, parts_ref[...], preferred_element_type=jnp.float32) + jnp.dot(
                low, parts_ref[...], preferred_element_type=jnp.float32
            )
            sums.append(part + pltpu.roll(part, k, 1))
        out_ref[rows, :] = jnp.where(lane < k, sums[0], sums[1])


def kept_kernel(packed_ref, basis_ref, old_ref, whole_ref):
    k = basis_ref.shape[1] // 2
    blocks = [packed_ref[i * k : (i + 1) * k] for i in range(6)]
    basis = basis_ref[...]
    for i in range(2):
        whole = put_whole(whole_ref, [x[:, i * k : (i + 1) * k] for x in blocks], k)
        old_ref[i * 2 * k : (i + 1) * 2 * k] = dot(basis, dot(whole, basis), TN)


def second_kernel(
    k,
    order,
    old_ref,
    fresh_ref,
    basis_ref,
    prod_ref,
    more_ref,
    r_ref,
    mix_ref,
    inv_ref,
    a_ref,
):
    def blocks(old, new):
        mid = new[k : 2 * k]
        return [
            old[:k, :k],
            new[:k].T,
            0.5 * (mid + mid.T),
            old[k:, :k],
            new[2 * k :],
            old[k:, k:],
        ]

    whole_a = put_whole(a_ref, blocks(old_ref[: 2 * k], fresh_ref[:, :k]), k)
    blocks_b = blocks(old_ref[2 * k :], fresh_ref[:, k:])
    coords, reduced = ritz_step(k, order, blocks_b, whole_a, inv_ref)
    basis = basis_ref[...]
    from_r = coords[k : 2 * k]
    move_p = dot(basis[:, k:], coords[2 * k :])
    move_x = dot(basis, jnp.concatenate([coords[:k], coords[2 * k :]], 0))
    more = more_ref[...].T
    mix_ref[: 3 * k] = jnp.concatenate([move_x, move_p], 1)
    mix_ref[3 * k :] = jnp.concatenate([from_r, from_r], 1)
    weights = jnp.concatenate(
        [move_x, -dot(move_x, reduced), from_r, -dot(from_r, reduced)], 0
    )
    vectors = jnp.concatenate([prod_ref[...], more], 0)
    resid = three(split(weights), split(vectors), TN)
    for i in range(r_ref.shape[0]):
        r_ref[i] = resid


def f32(*shape):
    return jax.ShapeDtypeStruct(shape, jnp.float32)


def cost(flops, size):
    return pl.CostEstimate(flops=int(flops), bytes_accessed=int(size), transcendentals=0)


def call(kernel, name, out_shape, scratch, flops, *args):
    return pl.pallas_call(
        kernel,
        out_shape=out_shape,
        scratch_shapes=[pltpu.VMEM(shape, jnp.float32) for shape in scratch],
        compiler_params=pltpu.CompilerParams(vmem_limit_bytes=32 * 2**20),
        cost_estimate=cost(flops, 2**20),
        name=name,
    )(*args)


def three(left, right, dims):
    def one(a, b):
        return lax.dot_general(a, b, (dims, ((), ())), preferred_element_type=jnp.float32)

    return one(left[0], right[1]) + one(left[1], right[0]) + one(left[0], right[0])


def products_kernel(x_ref, r_ref, p_ref, a_ref, b_ref, out_ref, panel_ref):
    k = x_ref.shape[0]
    wide = 3 * k

    @pl.when(pl.program_id(0) == 0)
    def _():
        for i, ref in enumerate((x_ref, r_ref, p_ref)):
            high, low = split(ref[...])
            panel_ref[i * k : (i + 1) * k] = high
            panel_ref[wide + i * k : wide + (i + 1) * k] = low

    def one(a, b):
        return jnp.dot(a, b, preferred_element_type=jnp.float32)

    for at, ref in ((0, a_ref), (wide, b_ref)):
        high, low = split(ref[...])
        both = one(panel_ref[...], high)
        prod = both[:wide] + both[wide:] + one(panel_ref[:wide], low)
        for i in range(out_ref.shape[0]):
            lanes = out_ref.shape[2]
            out_ref[i, at : at + wide] = prod[:, i * lanes : (i + 1) * lanes]


def gram_kernel(parts_ref, panel_ref, prods_ref, out_ref):
    wide = panel_ref.shape[0]
    k = wide // 3
    prods = parts_ref[0]
    for i in range(1, parts_ref.shape[0]):
        prods = prods + parts_ref[i]
    prods_ref[...] = prods
    gram = three(split(prods), split(panel_ref[...]), NT)
    at = 0
    for i in range(3):
        for j in range(i + 1):
            pair = []
            for base in (0, wide):
                block = gram[base + i * k : base + (i + 1) * k, j * k : (j + 1) * k]
                other = gram[base + j * k : base + (j + 1) * k, i * k : (i + 1) * k]
                pair.append(0.5 * (block + other.T))
            out_ref[at : at + k] = jnp.concatenate(pair, 1)
            at += k


def tests_kernel(turn_ref, prods_ref, basis_ref, own_ref, out_ref, resid_ref):
    k = turn_ref.shape[1]
    resid = dot(turn_ref[...], prods_ref[...], TN)
    resid_ref[:k] = resid
    resid_ref[k:] = jnp.zeros_like(resid)
    kept = dot(basis_ref[...], own_ref[...], TN)
    out_ref[:k] = kept[:k]
    out_ref[k : 2 * k] = resid
    out_ref[2 * k :] = kept[k:]


def fresh_kernel(parts_ref, tests_ref, more_ref, out_ref):
    more = parts_ref[0]
    for i in range(1, parts_ref.shape[0]):
        more = more + parts_ref[i]
    more_ref[...] = more
    out_ref[...] = three(split(tests_ref[...]), split(more), ((1,), (0,)))


def outputs_kernel(mix_ref, x_ref, r_ref, p_ref, resid_ref, x_out, p_out):
    k = x_ref.shape[0]
    resid = jnp.concatenate([resid_ref[i] for i in range(resid_ref.shape[0])], 1)
    vectors = jnp.concatenate([x_ref[...], r_ref[...], p_ref[...], resid], 0)
    out = three(split(mix_ref[...]), split(vectors), TN)
    x_out[...] = out[:k]
    p_out[...] = out[k:]


def products(x, r, p, a, b, pieces):
    k, rows = x.shape
    lanes = a.shape[1] // pieces
    each = 2
    block = pl.BlockSpec((k, rows), lambda i: (0, 0))
    tile = pl.BlockSpec((rows, each * lanes), lambda i: (0, i))
    return pl.pallas_call(
        products_kernel,
        grid=(pieces // each,),
        in_specs=[block, block, block, tile, tile],
        out_specs=pl.BlockSpec((each, 6 * k, lanes), lambda i: (i, 0, 0)),
        out_shape=f32(pieces, 6 * k, lanes),
        scratch_shapes=[pltpu.VMEM((6 * k, rows), jnp.bfloat16)],
        compiler_params=pltpu.CompilerParams(vmem_limit_bytes=60 * 2**20),
        cost_estimate=cost(1e10, 8 * rows * a.shape[1]),
        name="products",
    )(x, r, p, a, b)


def first_step(k, order, packed, prods, a, b):
    rows, cols = a.shape
    inside = pl.BlockSpec(memory_space=pltpu.VMEM)
    outside = pl.BlockSpec(memory_space=pl.ANY)
    return pl.pallas_call(
        functools.partial(first_kernel, k, order),
        in_specs=[inside, inside, outside, outside],
        out_specs=(inside, inside, inside),
        out_shape=(f32(6 * k, k), f32(3 * k, 2 * k), f32(rows, 2 * k)),
        scratch_shapes=[pltpu.VMEM((3 * k, 3 * k), jnp.float32)] * 2
        + [pltpu.VMEM((rows, cols), jnp.float32)] * 2
        + [pltpu.VMEM((cols, 2 * k), jnp.bfloat16)] * 2
        + [pltpu.SemaphoreType.DMA((2,))],
        compiler_params=pltpu.CompilerParams(vmem_limit_bytes=44 * 2**20),
        cost_estimate=cost(1.7e10, 8 * rows * cols),
        name="first_step",
    )(packed, prods, a, b)


def outputs(mix, x, r, p, resid):
    k, rows = x.shape
    pieces, _, lanes = resid.shape
    each = 8
    part = pl.BlockSpec((k, each * lanes), lambda i: (0, i))
    return pl.pallas_call(
        outputs_kernel,
        grid=(pieces // each,),
        in_specs=[
            pl.BlockSpec(mix.shape, lambda i: (0, 0)),
            part,
            part,
            part,
            pl.BlockSpec((each, k, lanes), lambda i: (i, 0, 0)),
        ],
        out_specs=(part, part),
        out_shape=(f32(k, rows), f32(k, rows)),
        compiler_params=pltpu.CompilerParams(vmem_limit_bytes=16 * 2**20),
        cost_estimate=cost(3e9, 40 * rows * k),
        name="outputs",
    )(mix, x, r, p, resid)


def local(a_matrix, b_matrix, x_block, r_block, p_block):
    rows, cols = lax.axis_size("row"), lax.axis_size("col")
    count = rows * cols
    k = x_block.shape[1]
    order = x_block.shape[0] * rows
    piece = order // count
    to_col = [(b, (b % rows) * cols + b // rows) for b in range(count)]
    to_row = [(d, s) for s, d in to_col]

    panel = [x_block.T, r_block.T, p_block.T]
    start = lax.axis_index("col") * piece
    own_row = jnp.concatenate(
        [lax.dynamic_slice_in_dim(x, start, piece, 1) for x in panel], 0
    )
    own_col = lax.ppermute(own_row, BOTH, to_col)

    prods = products(*panel, a_matrix, b_matrix, rows)
    prods = lax.all_to_all(prods, "row", 0, 0)
    prod_col, packed = call(
        gram_kernel, "gram", (f32(6 * k, piece), f32(6 * k, 2 * k)), [], 2e9, prods, own_col
    )
    prod_row = lax.ppermute(prod_col, BOTH, to_row)
    prods_col = lax.all_gather(prod_col, "row")
    packed = sum_everywhere(packed)
    turn, basis, parts = first_step(k, order, packed, prods_col, a_matrix, b_matrix)
    turn, prod_row, parts = lax.optimization_barrier((turn, prod_row, parts))
    parts = lax.all_to_all(parts.reshape(cols, piece, 2 * k), "col", 0, 0)
    old = call(kept_kernel, "kept", f32(4 * k, 2 * k), [(3 * k, 3 * k)], 3e9, packed, basis)
    tests, resid_row = call(
        tests_kernel,
        "tests",
        (f32(3 * k, piece), f32(2 * k, piece)),
        [],
        1e9,
        turn,
        prod_row,
        basis,
        own_row,
    )
    more_row, fresh = call(
        fresh_kernel, "fresh", (f32(piece, 2 * k), f32(3 * k, 2 * k)), [], 1e9, parts, tests
    )
    fresh, resid_row = lax.optimization_barrier((fresh, resid_row))
    resid = lax.all_gather(resid_row, "col")
    fresh = sum_everywhere(fresh)
    r_own, mix = call(
        functools.partial(second_kernel, k, order),
        "ritz_second",
        (f32(cols, k, piece), f32(4 * k, 2 * k)),
        [(3 * k, 3 * k)] * 2,
        1e7,
        old,
        fresh,
        basis,
        prod_row,
        more_row,
    )
    r_next = lax.all_to_all(r_own, "col", 0, 0)
    x_next, p_next = outputs(mix, *panel, resid)
    r_next, x_next, p_next = lax.optimization_barrier((r_next, x_next, p_next))
    r_next = r_next.transpose(1, 0, 2).reshape(k, -1)
    return (x_next.T, r_next.T, p_next.T)


def solution(mesh):
    return jax.shard_map(
        local,
        mesh=mesh,
        in_specs=(P("row", "col"), P("row", "col"), P("row", None), P("row", None), P("row", None)),
        out_specs=(P("row", None), P("row", None), P("row", None)),
        check_vma=False,
    )
```
